256 devices in a mesh: gx: 64 (over z_lo, x, y), gz: 4 (over z_hi, core).
Axes of the slice: x: 4, y: 4, z: 8 (z_hi: 2, z_lo: 4; z = z_hi * 4 + z_lo), core: 2. Of those that a mesh axis runs over, the one named last changes fastest.
Arguments:
- residual: float32 [1024, 512], P('gx', 'gz'), may hold values from -6 to 6
- whitening: float32 [1024, 512], P('gx', 'gz'), may hold values from 0.3 to 3
- kernel: float32 [256, 289], P('gz'), may hold values from -0.375 to 0.375
- adjoint_end: float32 [256, 1024, 512], P('gz', 'gx'), may hold values from -6 to 6
- pressure: bfloat16 [2, 256, 1024, 512], P(None, 'gz', 'gx'), may hold values from -6 to 6
- log_permeability: float32 [256, 1024, 512], P('gz', 'gx'), may hold values from -0.7 to 0.7
- vertical: bfloat16 [256, 1024, 512], P('gz', 'gx'), may hold values from 8 to 400
- top_layer: int32 [1024, 512], P('gx'), may hold values from 0 to 127
- well_columns: int32 [64], replicated, may hold values from 0 to 524287
Outputs:
- adjoint_start: float32 [256, 1024, 512], P('gz', 'gx')
- gradient: float32 [256, 1024, 512], P('gz', 'gx')
The draws below stay inside these ranges and needn't reach their ends.
Inputs may be any that keep to these rules, and one draw needn't show every extreme that they name: `well_columns`: indices may repeat.
All inputs are finite; a program needn't handle non-finite values.
Results may differ from the reference program's by a relative error of at most 0.0015.
Values may be sent and summed in bfloat16 or wider, within the bound.
A program may use at most 128 MiB of HBM per device.

```python
import math
import jax
import jax.numpy as jnp
from jax import lax

CX = 16
NY = 512
NZ = 256
KW = 17
NWELL = 64
NX = 1024
N_GX = 64


def with_ends(array, stream_key, low, high):
    spot = [jax.random.randint(jax.random.fold_in(stream_key, axis), (), 0, length) for axis, length in enumerate(array.shape)]
    longest = array.shape.index(max(array.shape))
    beside = spot[:longest] + [(spot[longest] + 1) % array.shape[longest]] + spot[longest + 1:]
    return array.at[tuple(spot)].set(low).at[tuple(beside)].set(high)


def shard_levels(key, shape, cuts, smallest, largest):
    gain, own = 1.0, jax.random.fold_in(key, 6)
    for axis_at, blocks in cuts:
        draws = jnp.exp(jax.random.uniform(jax.random.fold_in(own, axis_at), (blocks,), jnp.float32, smallest / len(cuts), largest / len(cuts)))
        gain = gain * jnp.repeat(draws, shape[axis_at] // blocks).reshape([-1 if axis == axis_at else 1 for axis in range(len(shape))])
    return gain


def scatter_about(key, extent, spread, reach, cuts=(), kind=jnp.bfloat16):
    array = jax.random.normal(key, extent, jnp.float32) * spread
    if len(cuts) > 0:
        array = shard_levels(key, extent, cuts, -0.22, 0.18) * array
    return jnp.clip(array, min=-reach, max=reach).astype(kind)


def setup_inputs(seed: int = 0) -> dict:
    arg_keys = jax.random.split(jax.random.key(seed), 10)
    residual = scatter_about(arg_keys[0], (NX, NY), 1.0, 6.0, ((0, 64), (1, 4)), jnp.float32)
    whitening = jnp.clip(jnp.exp(math.log(3.0) - 2.3025851 * jax.random.uniform(arg_keys[1], (NX, NY), jnp.float32) ** shard_levels(arg_keys[1], (NX, NY), ((0, 64), (1, 4)), -0.2, 0.2)), 0.3, 3.0)
    kernel = scatter_about(arg_keys[2], (NZ, KW * KW), (KW * KW) ** -0.5, 0.375, ((0, 4),), jnp.float32)
    adjoint_end = scatter_about(arg_keys[3], (NZ, NX, NY), 1.0, 6.0, ((0, 4), (1, 64)), jnp.float32)
    pressure = scatter_about(arg_keys[4], (2, NZ, NX, NY), 1.0, 6.0, ((1, 4), (2, 64)))
    log_permeability = jnp.clip(jax.random.uniform(arg_keys[5], (NZ, NX, NY), jnp.float32, -0.7, 0.7) * shard_levels(arg_keys[5], (NZ, NX, NY), ((0, 4), (1, 64)), -0.4, 0.0), -0.7, 0.7)
    vertical = jnp.clip(jnp.exp(math.log(400.0) - 3.912023 * jax.random.uniform(arg_keys[6], (NZ, NX, NY), jnp.float32) ** shard_levels(arg_keys[6], (NZ, NX, NY), ((0, 4), (1, 64)), -0.2, 0.2)), 8.0, 400.0).astype(jnp.bfloat16)
    top_layer = with_ends(jax.random.randint(arg_keys[7], (NX, NY), 0, NZ // 2), jax.random.fold_in(arg_keys[7], 1), 0, (NZ // 2) - 1).astype(jnp.int32)
    well_columns = with_ends(jax.random.randint(arg_keys[8], (NWELL,), 0, NX * NY), jax.random.fold_in(arg_keys[8], 1), 0, (NX * NY) - 1).astype(jnp.int32)
    return {"residual": residual, "whitening": whitening, "kernel": kernel, "adjoint_end": adjoint_end, "pressure": pressure, "log_permeability": log_permeability, "vertical": vertical, "top_layer": top_layer, "well_columns": well_columns}


STEP_SIZE = 0.1
KERNEL_HALF = 8
KERNEL_SIDE = 17


def neighbours(values):
    padded = jnp.pad(values, ((0, 0), (0, 0), (1, 1)))
    centre = padded[:, 1:-1, 1:-1]
    beside_all = (padded[:, 2:, 1:-1], padded[:, :-2, 1:-1], padded[:, 1:-1, 2:], padded[:, 1:-1, :-2])
    return centre, beside_all


def face_flux(adjoint_pad, mobility_pad, active_pad):
    adjoint_mid, adjoint_near = neighbours(adjoint_pad)
    mobility_mid, mobility_near = neighbours(mobility_pad)
    active_mid, active_near = neighbours(active_pad)
    summed = jnp.zeros_like(adjoint_mid)
    for adjoint_side, mobility_side, active_side in zip(adjoint_near, mobility_near, active_near):
        summed = summed + active_mid * active_side * 0.5 * (mobility_mid + mobility_side) * (adjoint_side - adjoint_mid)
    return summed


def misfit_term(adjoint_pad, pressure_pad, mobility_pad, active_pad):
    adjoint_mid, adjoint_near = neighbours(adjoint_pad)
    pressure_mid, pressure_near = neighbours(pressure_pad)
    mobility_mid, mobility_near = neighbours(mobility_pad)
    active_mid, active_near = neighbours(active_pad)
    summed = jnp.zeros_like(adjoint_mid)
    for adjoint_side, pressure_side, active_side in zip(adjoint_near, pressure_near, active_near):
        summed = summed + active_side * (adjoint_side - adjoint_mid) * (pressure_side - pressure_mid)
    return STEP_SIZE * 0.5 * active_mid * mobility_mid * summed


def vertical_solve(explicit, vertical, active):
    divisor = 1.0 + vertical
    factor = active * vertical / divisor
    addend = active * explicit / divisor

    def layer_step(below, pieces):
        factor_z, addend_z = pieces
        solved_z = factor_z * below + addend_z
        return solved_z, solved_z

    starting = jnp.zeros(explicit.shape[1:], jnp.float32)
    _, solved = lax.scan(layer_step, starting, (factor, addend), reverse=True)
    return solved


def reference(residual, whitening, kernel, adjoint_end, pressure, log_permeability, vertical, top_layer, well_columns):
    whitened = residual * whitening
    padded_surface = jnp.pad(whitened, ((KERNEL_HALF, KERNEL_HALF), (KERNEL_HALF, KERNEL_HALF)))

    def column_block(start):
        window = lax.dynamic_slice_in_dim(padded_surface, start, CX + 2 * KERNEL_HALF, 0)
        patches = jnp.stack([window[shift_x:shift_x + CX, shift_y:shift_y + NY]
                             for shift_x in range(KERNEL_SIDE) for shift_y in range(KERNEL_SIDE)])
        product = jnp.dot(kernel, patches.reshape(KERNEL_SIDE * KERNEL_SIDE, CX * NY),
                          precision=lax.Precision.HIGHEST, preferred_element_type=jnp.float32)
        return product.reshape(NZ, CX, NY)

    starts = (jnp.arange(N_GX, dtype=jnp.int32) * CX).astype(jnp.int32)
    blocks = lax.map(column_block, starts)
    source = jnp.transpose(blocks, (1, 0, 2, 3)).reshape(NZ, NX, NY)
    columns = jnp.ones((NX * NY,), jnp.float32).at[well_columns].set(0.0).reshape(NX, NY)
    layer_ids = jnp.arange(NZ, dtype=jnp.int32)[:, None, None]
    active = jnp.where(layer_ids >= top_layer[None], columns[None], jnp.zeros((), jnp.float32))
    mobility = jnp.exp(log_permeability)
    vertical_f = vertical.astype(jnp.float32)

    def pad_x(values):
        return jnp.pad(values, ((0, 0), (1, 1), (0, 0)))

    mobility_pad = pad_x(mobility)
    active_pad = pad_x(active)
    adjoint = adjoint_end
    gradient = jnp.zeros_like(adjoint_end)
    for time_level in range(2):
        adjoint_pad = pad_x(adjoint)
        pressure_pad = pad_x(pressure[time_level].astype(jnp.float32))
        gradient = gradient + misfit_term(adjoint_pad, pressure_pad, mobility_pad, active_pad)
        explicit = adjoint + STEP_SIZE * face_flux(adjoint_pad, mobility_pad, active_pad) + source
        adjoint = vertical_solve(explicit, vertical_f, active)
    return adjoint, gradient
```

```python
import functools

import jax
import jax.numpy as jnp
from jax import lax
from jax.experimental import pallas as pl
from jax.experimental.pallas import tpu as pltpu
from jax.sharding import PartitionSpec as P

STEP_SIZE = 0.1
HALF = 8
SIDE = 17
FAR = 1e6
MESH = pl.DeviceIdType.MESH
CHUNKS = 4
LANES = 128


def get(ref, at):
    return jnp.concatenate([ref[q, at, :] for q in range(ref.shape[0])], axis=1)


def put(ref, at, value):
    for q in range(ref.shape[0]):
        ref[q, at, :] = value[:, q * LANES : (q + 1) * LANES]


def window_kernel(
    n_gx,
    n_gz,
    depth,
    cols,
    rows,
    residual_ref,
    whitening_ref,
    kernel_ref,
    top_ref,
    wells_ref,
    adjoint_hbm,
    pressure_hbm,
    logk_hbm,
    vertical_hbm,
    out_hbm,
    grad_hbm,
    adj,
    prs,
    mob,
    ver,
    tx,
    ty,
    exp_,
    rec,
    dec,
    mid,
    src,
    gsum,
    fin,
    surf,
    shifted,
    rhs_hi,
    rhs_lo,
    kpad,
    toep,
    tops,
    send_halo,
    recv_halo,
    send_top,
    recv_top,
    send_mid,
    recv_mid,
    send_inc,
    recv_inc,
    load_sem,
    store_sem,
    surf_send,
    surf_recv,
    edge_send,
    edge_recv,
    halo_send,
    halo_recv,
    top_send,
    top_recv,
    mid_send,
    mid_recv,
    inc_send,
    inc_recv,
):
    gx = lax.axis_index("gx")
    gz = lax.axis_index("gz")
    layers = depth // CHUNKS
    span = layers * cols
    has = (gx > 0, gx < n_gx - 1)
    beside = (gx - 1, gx + 1)

    def loads(c):
        at = c * span
        here = pl.ds(at, span)
        there = pl.ds(depth * cols + at, span)
        pairs = [
            (pressure_hbm.at[here], prs.at[here]),
            (pressure_hbm.at[there], prs.at[there]),
        ]
        for q in range(rows // LANES):
            lane = pl.ds(q * LANES, LANES)
            pairs.append((adjoint_hbm.at[here, lane], adj.at[q, here]))
            pairs.append((logk_hbm.at[here, lane], mob.at[q, here]))
        pairs.append((vertical_hbm.at[here], ver.at[here]))
        return [
            pltpu.make_async_copy(a, b, load_sem.at[c, i]) for i, (a, b) in enumerate(pairs)
        ]

    for c in reversed(range(CHUNKS)):
        for copy in loads(c):
            copy.start()

    barrier = pltpu.get_barrier_semaphore()
    for j in range(1, n_gz):
        pl.semaphore_signal(
            barrier, inc=1, device_id=(gx, lax.rem(gz + j, n_gz)), device_id_type=MESH
        )
    for s in range(2):

        @pl.when(has[s])
        def _():
            pl.semaphore_signal(barrier, inc=1, device_id=(beside[s], gz), device_id_type=MESH)

    strip = surf.at[gz]
    strip[HALF : HALF + cols, :] = residual_ref[...] * whitening_ref[...]
    for s in range(2):

        @pl.when(jnp.logical_not(has[s]))
        def _():
            first = s * (HALF + cols)
            surf[:, first : first + HALF, :] = jnp.zeros((n_gz, HALF, rows // n_gz), jnp.float32)
            recv_halo[s] = jnp.zeros(recv_halo.shape[1:], recv_halo.dtype)
            recv_top[s] = jnp.full(recv_top.shape[1:], FAR, jnp.float32)
            recv_mid[s] = jnp.zeros(recv_mid.shape[1:], recv_mid.dtype)

    @pl.when(gz == n_gz - 1)
    def _():
        recv_inc[...] = jnp.zeros(recv_inc.shape, jnp.float32)

    cell = (
        (gx * cols + lax.broadcasted_iota(jnp.int32, (cols, rows), 0)) * rows
        + lax.broadcasted_iota(jnp.int32, (cols, rows), 1)
    )

    def drill(i, top):
        return jnp.where(cell == wells_ref[i], FAR, top)

    top = lax.fori_loop(0, wells_ref.shape[0], drill, top_ref[...].astype(jnp.float32))
    x_id = lax.broadcasted_iota(jnp.int32, (cols, rows), 0)
    y_id = lax.broadcasted_iota(jnp.int32, (cols, rows), 1)
    tops[0] = top
    tops[1] = jnp.where(x_id == cols - 1, FAR, jnp.maximum(top, pltpu.roll(top, cols - 1, 0)))
    tops[2] = jnp.where(y_id == rows - 1, FAR, jnp.maximum(top, pltpu.roll(top, rows - 1, 1)))
    send_top[0] = jnp.broadcast_to(top[0:1, :], (8, rows))
    send_top[1] = jnp.broadcast_to(top[cols - 1 : cols, :], (8, rows))

    kpad[...] = jnp.zeros(kpad.shape, jnp.float32)
    kpad[:, 0 : SIDE * SIDE] = kernel_ref[...]
    for x in range(8):
        put(toep, pl.ds(x, depth, stride=8), pltpu.roll(kpad[...], SIDE * x, 1))
    tail = shifted.shape[1] - (cols + 2 * HALF) * SIDE
    put(shifted, pl.ds((cols + 2 * HALF) * SIDE, tail), jnp.zeros((tail, rows), jnp.float32))

    strips_beside = jnp.where(has[0], 1, 0) + jnp.where(has[1], 1, 0)
    pl.semaphore_wait(barrier, n_gz - 1 + strips_beside)

    def surf_copy(j):
        mine = surf.at[gz, pl.ds(HALF, cols), :]
        return pltpu.make_async_remote_copy(
            src_ref=mine,
            dst_ref=mine,
            send_sem=surf_send.at[j - 1],
            recv_sem=surf_recv.at[j - 1],
            device_id=(gx, lax.rem(gz + j, n_gz)),
            device_id_type=MESH,
        )

    for j in range(1, n_gz):
        surf_copy(j).start()

    def select_rows(side_col):
        z_of = lax.broadcasted_iota(jnp.int32, (16, 256), 0)
        k_of = lax.broadcasted_iota(jnp.int32, (16, 256), 1)
        return (k_of == z_of * cols + side_col).astype(jnp.bfloat16)

    for c in reversed(range(CHUNKS)):
        for copy in loads(c):
            copy.wait()

    def pack(i, carry):
        z0 = pl.multiple_of(i * 16, 16)
        r0 = pl.multiple_of(i * 16 * cols, 16 * cols)
        for s in range(2):
            x = s * (cols - 1)
            line = pl.ds(r0 + x, 16, stride=cols)
            send_halo[s, pl.ds(z0, 16), :] = get(adj, line).astype(jnp.bfloat16)
            send_halo[s, pl.ds(depth + z0, 16), :] = jnp.exp(get(mob, line)).astype(jnp.bfloat16)
            pick = select_rows(x)
            for k in range(2):
                block = prs[pl.ds(k * depth * cols + r0, 16 * cols), :]
                send_halo[s, pl.ds((2 + k) * depth + z0, 16), :] = jnp.dot(
                    pick, block, preferred_element_type=jnp.float32
                ).astype(jnp.bfloat16)
        return carry

    lax.fori_loop(0, depth // 16, pack, 0)

    def side_copies(s):
        out = []
        for a, b, ss, rs in (
            (send_top, recv_top, top_send, top_recv),
            (send_halo, recv_halo, halo_send, halo_recv),
        ):
            out.append(
                pltpu.make_async_remote_copy(
                    src_ref=a.at[s],
                    dst_ref=b.at[1 - s],
                    send_sem=ss.at[s],
                    recv_sem=rs.at[1 - s],
                    device_id=(beside[s], gz),
                    device_id_type=MESH,
                )
            )
        return out

    def side_arrivals(s):
        return [
            pltpu.make_async_remote_copy(
                src_ref=a.at[1 - s],
                dst_ref=b.at[s],
                send_sem=ss.at[1 - s],
                recv_sem=rs.at[s],
                device_id=(beside[s], gz),
                device_id_type=MESH,
            )
            for a, b, ss, rs in (
                (send_top, recv_top, top_send, top_recv),
                (send_halo, recv_halo, halo_send, halo_recv),
            )
        ]

    for s in range(2):

        @pl.when(has[s])
        def _():
            for copy in side_copies(s):
                copy.start()

    z_base = gz * depth

    def faces(value, back):
        return value - pltpu.roll(value, back, 0)

    def lateral(z, a, p, tface_x, tface_y, zf):
        dx = jnp.where(tops[1] <= zf, pltpu.roll(a, cols - 1, 0) - a, 0.0)
        gxx = dx * (pltpu.roll(p, cols - 1, 0) - p)
        fx = tface_x * dx
        dy = jnp.where(tops[2] <= zf, pltpu.roll(a, rows - 1, 1) - a, 0.0)
        gyy = dy * (pltpu.roll(p, rows - 1, 1) - p)
        fy = tface_y * dy
        flux = (fx - pltpu.roll(fx, 1, 0)) + (fy - pltpu.roll(fy, 1, 1))
        term = (gxx + pltpu.roll(gxx, 1, 0)) + (gyy + pltpu.roll(gyy, 1, 1))
        return flux, term

    def first_layer(i, decay):
        z = depth - 1 - i
        here = pl.ds(pl.multiple_of(z * cols, cols), cols)
        zf = (z_base + z).astype(jnp.float32)
        m = jnp.exp(get(mob, here))
        put(mob, here, m)
        half_m = (0.5 * STEP_SIZE) * m
        tface_x = half_m + pltpu.roll(half_m, cols - 1, 0)
        tface_y = half_m + pltpu.roll(half_m, rows - 1, 1)
        tx[here, :] = tface_x
        ty[here, :] = tface_y
        a = get(adj, here)
        flux, term = lateral(z, a, prs[here, :].astype(jnp.float32), tface_x, tface_y, zf)
        put(exp_, here, a + flux)
        put(gsum, here, term)
        r = 1.0 / (1.0 + ver[here, :].astype(jnp.float32))
        rec[here, :] = r
        decay = jnp.where(tops[0] <= zf, decay - r * decay, 0.0)
        put(dec, here, decay)
        return decay

    decay = jnp.ones((cols, rows), jnp.float32)
    decay = lax.fori_loop(0, depth // 2, first_layer, decay)

    def edge_copy(s):
        first = HALF + s * (cols - HALF)
        return pltpu.make_async_remote_copy(
            src_ref=surf.at[:, pl.ds(first, HALF), :],
            dst_ref=surf.at[:, pl.ds((1 - s) * (HALF + cols), HALF), :],
            send_sem=edge_send.at[s],
            recv_sem=edge_recv.at[1 - s],
            device_id=(beside[s], gz),
            device_id_type=MESH,
        )

    def edge_arrival(s):
        first = HALF + (1 - s) * (cols - HALF)
        return pltpu.make_async_remote_copy(
            src_ref=surf.at[:, pl.ds(first, HALF), :],
            dst_ref=surf.at[:, pl.ds(s * (HALF + cols), HALF), :],
            send_sem=edge_send.at[1 - s],
            recv_sem=edge_recv.at[s],
            device_id=(beside[s], gz),
            device_id_type=MESH,
        )

    def surf_arrival(j):
        theirs = surf.at[lax.rem(gz + n_gz - j, n_gz), pl.ds(HALF, cols), :]
        return pltpu.make_async_remote_copy(
            src_ref=theirs,
            dst_ref=theirs,
            send_sem=surf_send.at[j - 1],
            recv_sem=surf_recv.at[j - 1],
            device_id=(gx, lax.rem(gz + j, n_gz)),
            device_id_type=MESH,
        )

    for j in range(1, n_gz):
        surf_arrival(j).wait_recv()
    for s in range(2):

        @pl.when(has[s])
        def _():
            edge_copy(s).start()

    lax.fori_loop(depth // 2, depth, first_layer, decay)

    for s in range(2):

        @pl.when(has[s])
        def _():
            edge_arrival(s).wait_recv()

    surface = jnp.concatenate([surf[g] for g in range(n_gz)], axis=1)
    wide_y = lax.broadcasted_iota(jnp.int32, surface.shape, 1)
    for b in range(SIDE):
        off = b - HALF
        turned = surface if off == 0 else pltpu.roll(surface, (-off) % rows, 1)
        if off > 0:
            turned = jnp.where(wide_y < rows - off, turned, 0.0)
        if off < 0:
            turned = jnp.where(wide_y >= -off, turned, 0.0)
        put(shifted, pl.ds(b, cols + 2 * HALF, stride=SIDE), turned)
    for h in range(2):
        for q in range(4):
            piece = get(shifted, pl.ds(h * 8 * SIDE + q * 128, 128))
            hi = piece.astype(jnp.bfloat16)
            rhs_hi[h, pl.ds(q * 128, 128), :] = hi
            rhs_lo[h, pl.ds(q * 128, 128), :] = (piece - hi.astype(jnp.float32)).astype(
                jnp.bfloat16
            )

    def product(i, carry):
        tile = pl.ds(pl.multiple_of(i * 128, 128), 128)
        lhs = get(toep, tile)
        hi = lhs.astype(jnp.bfloat16)
        lo = (lhs - hi.astype(jnp.float32)).astype(jnp.bfloat16)
        for h in range(2):
            src[h, tile, :] = (
                jnp.dot(hi, rhs_hi[h], preferred_element_type=jnp.float32)
                + jnp.dot(hi, rhs_lo[h], preferred_element_type=jnp.float32)
                + jnp.dot(lo, rhs_hi[h], preferred_element_type=jnp.float32)
            )
        return carry

    lax.fori_loop(0, depth * 8 // 128, product, 0)

    for s in range(2):

        @pl.when(has[s])
        def _():
            for copy in side_arrivals(s):
                copy.wait_recv()

    def edges(state, arrived, level):
        def step(i, carry):
            z0 = pl.multiple_of(i * 16, 16)
            r0 = pl.multiple_of(i * 16 * cols, 16 * cols)
            zf = (z_base + z0 + lax.broadcasted_iota(jnp.int32, (16, rows), 0)).astype(jnp.float32)
            for s in range(2):
                x = s * (cols - 1)
                line = pl.ds(r0 + x, 16, stride=cols)
                near = get(state, line)
                far = arrived[s, pl.ds(z0, 16), :].astype(jnp.float32)
                far_m = recv_halo[s, pl.ds(depth + z0, 16), :].astype(jnp.float32)
                far_p = recv_halo[s, pl.ds((2 + level) * depth + z0, 16), :].astype(jnp.float32)
                near_p = send_halo[s, pl.ds((2 + level) * depth + z0, 16), :].astype(jnp.float32)
                face = jnp.maximum(tops[0, x : x + 1, :], recv_top[s, 0:1, :])
                d = jnp.where(face <= zf, far - near, 0.0)
                flux = (0.5 * STEP_SIZE) * (get(mob, line) + far_m) * d
                put(exp_, line, get(exp_, line) + flux)
                put(gsum, line, get(gsum, line) + d * (far_p - near_p))
            return carry

        lax.fori_loop(0, depth // 16, step, 0)

    edges(adj, recv_halo, 0)

    def split(z):
        r = pl.multiple_of(z * cols, cols)
        return [pl.ds(r, 8), pl.ds(pl.multiple_of(r + 8, 8), 8)]

    def chain_first(i, below):
        z = depth - 1 - i
        zf = (z_base + z).astype(jnp.float32)
        eight = pl.ds(pl.multiple_of(z * 8, 8), 8)
        solved = []
        for h, part in enumerate(split(z)):
            e = get(exp_, part) + src[h, eight, :]
            v = jnp.where(
                tops[0, 8 * h : 8 * h + 8, :] <= zf, below[h] + rec[part, :] * (e - below[h]), 0.0
            )
            put(mid, part, v)
            solved.append(v)
        return tuple(solved)

    nothing = (jnp.zeros((8, rows), jnp.float32),) * 2
    lax.fori_loop(0, depth, chain_first, nothing)

    def inc_copy(level):
        return pltpu.make_async_remote_copy(
            src_ref=send_inc.at[level],
            dst_ref=recv_inc.at[level],
            send_sem=inc_send.at[level],
            recv_sem=inc_recv.at[level],
            device_id=(gx, gz - 1),
            device_id_type=MESH,
        )

    def inc_arrival(level):
        return pltpu.make_async_remote_copy(
            src_ref=send_inc.at[level],
            dst_ref=recv_inc.at[level],
            send_sem=inc_send.at[level],
            recv_sem=inc_recv.at[level],
            device_id=(gx, gz + 1),
            device_id_type=MESH,
        )

    def relay(level):
        @pl.when(gz < n_gz - 1)
        def _():
            inc_arrival(level).wait_recv()

        @pl.when(gz > 0)
        def _():
            first = pl.ds(0, cols)
            send_inc[level] = get(mid, first) + get(dec, first) * recv_inc[level]
            inc_copy(level).start()

    relay(0)

    def pack_mid(i, carry):
        z0 = pl.multiple_of(i * 16, 16)
        r0 = pl.multiple_of(i * 16 * cols, 16 * cols)
        for s in range(2):
            x = s * (cols - 1)
            line = pl.ds(r0 + x, 16, stride=cols)
            send_mid[s, pl.ds(z0, 16), :] = (
                get(mid, line) + get(dec, line) * recv_inc[0, x : x + 1, :]
            ).astype(jnp.bfloat16)
        return carry

    lax.fori_loop(0, depth // 16, pack_mid, 0)

    def mid_copy(s):
        return pltpu.make_async_remote_copy(
            src_ref=send_mid.at[s],
            dst_ref=recv_mid.at[1 - s],
            send_sem=mid_send.at[s],
            recv_sem=mid_recv.at[1 - s],
            device_id=(beside[s], gz),
            device_id_type=MESH,
        )

    def mid_arrival(s):
        return pltpu.make_async_remote_copy(
            src_ref=send_mid.at[1 - s],
            dst_ref=recv_mid.at[s],
            send_sem=mid_send.at[1 - s],
            recv_sem=mid_recv.at[s],
            device_id=(beside[s], gz),
            device_id_type=MESH,
        )

    for s in range(2):

        @pl.when(has[s])
        def _():
            mid_copy(s).start()

    def second_layer(i, carry):
        z = depth - 1 - i
        here = pl.ds(pl.multiple_of(z * cols, cols), cols)
        there = pl.ds(pl.multiple_of((depth + z) * cols, cols), cols)
        eight = pl.ds(pl.multiple_of(z * 8, 8), 8)
        zf = (z_base + z).astype(jnp.float32)
        a = get(mid, here) + get(dec, here) * recv_inc[0]
        put(mid, here, a)
        flux, term = lateral(
            z, a, prs[there, :].astype(jnp.float32), tx[here, :], ty[here, :], zf
        )
        source = jnp.concatenate([src[0, eight, :], src[1, eight, :]], axis=0)
        put(exp_, here, a + flux + source)
        put(gsum, here, get(gsum, here) + term)
        return carry

    lax.fori_loop(0, depth, second_layer, 0)

    for s in range(2):

        @pl.when(has[s])
        def _():
            mid_arrival(s).wait_recv()

    edges(mid, recv_mid, 1)

    def chain_second(i, below):
        z = depth - 1 - i
        here = pl.ds(pl.multiple_of(z * cols, cols), cols)
        zf = (z_base + z).astype(jnp.float32)
        v = jnp.where(tops[0] <= zf, below + rec[here, :] * (get(exp_, here) - below), 0.0)
        put(mid, here, v)
        put(gsum, here, (0.5 * STEP_SIZE) * get(mob, here) * get(gsum, here))
        return v

    lax.fori_loop(0, depth, chain_second, jnp.zeros((cols, rows), jnp.float32))

    def grad_copy(q):
        lane = pl.ds(q * LANES, LANES)
        return pltpu.make_async_copy(
            gsum.at[q], grad_hbm.at[:, lane], store_sem.at[CHUNKS + q]
        )

    for q in range(rows // LANES):
        grad_copy(q).start()
    relay(1)

    def finish(i, carry):
        here = pl.ds(pl.multiple_of(i * cols, cols), cols)
        fin[here, :] = get(mid, here) + get(dec, here) * recv_inc[1]
        return carry

    def store(c):
        part = pl.ds(c * span, span)
        return pltpu.make_async_copy(fin.at[part], out_hbm.at[part], store_sem.at[c])

    for c in range(CHUNKS):
        lax.fori_loop(c * layers, (c + 1) * layers, finish, 0)
        store(c).start()

    for j in range(1, n_gz):
        surf_copy(j).wait_send()
    for s in range(2):

        @pl.when(has[s])
        def _():
            for copy in side_copies(s):
                copy.wait_send()
            edge_copy(s).wait_send()
            mid_copy(s).wait_send()

    @pl.when(gz > 0)
    def _():
        inc_copy(0).wait_send()
        inc_copy(1).wait_send()

    for q in range(rows // LANES):
        grad_copy(q).wait()
    for c in range(CHUNKS):
        store(c).wait()


def on_device(
    n_gx,
    n_gz,
    residual,
    whitening,
    kernel,
    adjoint_end,
    pressure,
    log_permeability,
    vertical,
    top_layer,
    well_columns,
):
    depth, cols, rows = adjoint_end.shape
    cells = depth * cols
    f32, b16 = jnp.float32, jnp.bfloat16
    field = pltpu.VMEM((cells, rows), f32)
    lanes = rows // LANES
    banded = pltpu.VMEM((lanes, cells, LANES), f32)
    dma = pltpu.SemaphoreType.DMA
    wide = cols + 2 * HALF
    vmem = pl.BlockSpec(memory_space=pltpu.VMEM)
    smem = pl.BlockSpec(memory_space=pltpu.SMEM)
    hbm = pl.BlockSpec(memory_space=pl.ANY)
    adjoint_start, gradient = pl.pallas_call(
        functools.partial(window_kernel, n_gx, n_gz, depth, cols, rows),
        out_shape=(jax.ShapeDtypeStruct((cells, rows), f32),) * 2,
        in_specs=[vmem, vmem, vmem, vmem, smem, hbm, hbm, hbm, hbm],
        out_specs=(hbm, hbm),
        scratch_shapes=[
            banded,
            pltpu.VMEM((2 * cells, rows), b16),
            banded,
            pltpu.VMEM((cells, rows), b16),
            field,
            field,
            banded,
            field,
            banded,
            banded,
            pltpu.VMEM((2, depth * 8, rows), f32),
            banded,
            field,
            pltpu.VMEM((n_gz, wide, rows // n_gz), f32),
            pltpu.VMEM((lanes, 8 * SIDE + 512, LANES), f32),
            pltpu.VMEM((2, 512, rows), b16),
            pltpu.VMEM((2, 512, rows), b16),
            pltpu.VMEM((depth, 512), f32),
            pltpu.VMEM((4, depth * 8, LANES), f32),
            pltpu.VMEM((3, cols, rows), f32),
            pltpu.VMEM((2, 4 * depth, rows), b16),
            pltpu.VMEM((2, 4 * depth, rows), b16),
            pltpu.VMEM((2, 8, rows), f32),
            pltpu.VMEM((2, 8, rows), f32),
            pltpu.VMEM((2, depth, rows), b16),
            pltpu.VMEM((2, depth, rows), b16),
            pltpu.VMEM((2, cols, rows), f32),
            pltpu.VMEM((2, cols, rows), f32),
            dma((CHUNKS, 3 + 2 * lanes)),
            dma((lanes + CHUNKS,)),
            dma((n_gz - 1,)),
            dma((n_gz - 1,)),
        ]
        + [dma((2,))] * 10,
        compiler_params=pltpu.CompilerParams(
            collective_id=0, has_side_effects=True, vmem_limit_bytes=56 * 1024 * 1024
        ),
    )(
        residual,
        whitening,
        kernel,
        top_layer,
        well_columns,
        adjoint_end.reshape(cells, rows),
        pressure.reshape(2 * cells, rows),
        log_permeability.reshape(cells, rows),
        vertical.reshape(cells, rows),
    )
    shape = (depth, cols, rows)
    return adjoint_start.reshape(shape), gradient.reshape(shape)


def solution(mesh):
    in_specs = (
        P("gx", "gz"),
        P("gx", "gz"),
        P("gz", None),
        P("gz", "gx", None),
        P(None, "gz", "gx", None),
        P("gz", "gx", None),
        P("gz", "gx", None),
        P("gx", None),
        P(),
    )
    out_specs = (P("gz", "gx", None), P("gz", "gx", None))
    return jax.shard_map(
        functools.partial(on_device, mesh.shape["gx"], mesh.shape["gz"]),
        mesh=mesh,
        in_specs=in_specs,
        out_specs=out_specs,
        check_vma=False,
    )
```

```python
import functools

import jax
import jax.numpy as jnp
from jax import lax
from jax.experimental import pallas as pl
from jax.experimental.pallas import tpu as pltpu
from jax.sharding import PartitionSpec as P

STEP_SIZE = 0.1
HALF = 8
SIDE = 17
FAR = 1e6
MESH = pl.DeviceIdType.MESH
CHUNKS = 2
UNROLL = 4
LANES = 128


def get(ref, at):
    return jnp.concatenate([ref[q, at, :] for q in range(ref.shape[0])], axis=1)


def put(ref, at, value):
    for q in range(ref.shape[0]):
        ref[q, at, :] = value[:, q * LANES : (q + 1) * LANES]


def every(low, high, unroll, body):
    def step(i, carry):
        body(i)
        return carry

    lax.fori_loop(low, high, step, 0, unroll=unroll)


def window_kernel(
    n_gx,
    n_gz,
    depth,
    cols,
    rows,
    residual_hbm,
    whitening_hbm,
    kernel_hbm,
    top_hbm,
    wells_hbm,
    adjoint_hbm,
    pressure_hbm,
    logk_hbm,
    vertical_hbm,
    out_ref,
    grad_ref,
    residual_ref,
    whitening_ref,
    kernel_ref,
    top_ref,
    wells_ref,
    adj,
    prs,
    mob,
    ver,
    tx,
    ty,
    fx,
    gx_sum,
    gy_sum,
    part_exp,
    steps_y,
    rec,
    fac,
    dec,
    low,
    mid,
    src,
    surf,
    shifted,
    rhs_hi,
    rhs_lo,
    kpad,
    toep,
    toep_hi,
    toep_lo,
    tops,
    near_adj,
    near_mob,
    edge_flux,
    edge_term,
    send_halo,
    recv_halo,
    send_prs,
    recv_prs,
    send_top,
    recv_top,
    send_mid,
    recv_mid,
    send_inc,
    recv_inc,
    small_sem,
    load_sem,
    surf_send,
    surf_recv,
    edge_send,
    edge_recv,
    halo_send,
    halo_recv,
    prs_send,
    prs_recv,
    top_send,
    top_recv,
    mid_send,
    mid_recv,
    inc_send,
    inc_recv,
):
    gx = lax.axis_index("gx")
    gz = lax.axis_index("gz")
    layers = depth // CHUNKS
    span = layers * cols
    cells = depth * cols
    bands = rows // LANES
    has = (gx > 0, gx < n_gx - 1)
    beside = (gx - 1, gx + 1)

    barrier = pltpu.get_barrier_semaphore()
    for j in range(1, n_gz):
        pl.semaphore_signal(
            barrier, inc=1, device_id=(gx, lax.rem(gz + j, n_gz)), device_id_type=MESH
        )
    for s in range(2):

        @pl.when(has[s])
        def _():
            pl.semaphore_signal(barrier, inc=1, device_id=(beside[s], gz), device_id_type=MESH)

    small = [
        pltpu.make_async_copy(a, b, small_sem.at[i])
        for i, (a, b) in enumerate(
            (
                (residual_hbm, residual_ref),
                (whitening_hbm, whitening_ref),
                (top_hbm, top_ref),
                (wells_hbm, wells_ref),
                (kernel_hbm, kernel_ref),
            )
        )
    ]
    for copy in small:
        copy.start()

    def loads(c):
        at = c * span
        here = pl.ds(at, span)
        pairs = []
        for q in range(bands):
            lane = pl.ds(q * LANES, LANES)
            pairs.append((logk_hbm.at[here, lane], mob.at[q, here]))
            pairs.append((adjoint_hbm.at[here, lane], adj.at[q, here]))
        pairs.append((vertical_hbm.at[here], ver.at[here]))
        return [
            pltpu.make_async_copy(a, b, load_sem.at[c, i]) for i, (a, b) in enumerate(pairs)
        ]

    chunk_loads = [loads(c) for c in range(CHUNKS)]
    for copies in reversed(chunk_loads):
        for copy in copies[: 2 * bands]:
            copy.start()
    for copies in reversed(chunk_loads):
        copies[2 * bands].start()
    load_prs = pltpu.make_async_copy(pressure_hbm, prs, small_sem.at[5])
    load_prs.start()

    for s in range(2):

        @pl.when(jnp.logical_not(has[s]))
        def _():
            first = s * (HALF + cols)
            surf[:, first : first + HALF, :] = jnp.zeros((n_gz, HALF, rows // n_gz), jnp.float32)
            recv_halo[s] = jnp.zeros(recv_halo.shape[1:], recv_halo.dtype)
            recv_top[s] = jnp.full(recv_top.shape[1:], FAR, jnp.float32)
            recv_mid[s] = jnp.zeros(recv_mid.shape[1:], recv_mid.dtype)
            recv_prs[s] = jnp.zeros(recv_prs.shape[1:], recv_prs.dtype)

    @pl.when(gz == n_gz - 1)
    def _():
        recv_inc[...] = jnp.zeros(recv_inc.shape, jnp.float32)

    blank = jnp.zeros((8, rows), jnp.float32)
    after = pl.ds(cells, 8)
    for ref in (mob, adj, low, dec, mid):
        put(ref, after, blank)
    for ref in (fx, gx_sum):
        put(ref, pl.ds(0, 8), blank)

    small[0].wait()
    small[1].wait()
    strip = surf.at[gz]
    strip[HALF : HALF + cols, :] = residual_ref[...] * whitening_ref[...]

    small[2].wait()
    small[3].wait()
    cell = (
        (gx * cols + lax.broadcasted_iota(jnp.int32, (cols, rows), 0)) * rows
        + lax.broadcasted_iota(jnp.int32, (cols, rows), 1)
    )

    def drill(i, top):
        return jnp.where(cell == wells_ref[i], FAR, top)

    top = lax.fori_loop(
        0, wells_ref.shape[0], drill, top_ref[...].astype(jnp.float32), unroll=8
    )
    x_id = lax.broadcasted_iota(jnp.int32, (cols, rows), 0)
    y_id = lax.broadcasted_iota(jnp.int32, (cols, rows), 1)
    tops[0] = top
    tops[1] = jnp.where(x_id == cols - 1, FAR, jnp.maximum(top, pltpu.roll(top, cols - 1, 0)))
    tops[2] = jnp.where(y_id == rows - 1, FAR, jnp.maximum(top, pltpu.roll(top, rows - 1, 1)))
    send_top[0] = jnp.broadcast_to(top[0:1, :], (8, rows))
    send_top[1] = jnp.broadcast_to(top[cols - 1 : cols, :], (8, rows))

    strips_beside = jnp.where(has[0], 1, 0) + jnp.where(has[1], 1, 0)
    pl.semaphore_wait(barrier, n_gz - 1 + strips_beside)

    def surf_copy(j):
        mine = surf.at[gz, pl.ds(HALF, cols), :]
        return pltpu.make_async_remote_copy(
            src_ref=mine,
            dst_ref=mine,
            send_sem=surf_send.at[j - 1],
            recv_sem=surf_recv.at[j - 1],
            device_id=(gx, lax.rem(gz + j, n_gz)),
            device_id_type=MESH,
        )

    def surf_arrival(j):
        theirs = surf.at[lax.rem(gz + n_gz - j, n_gz), pl.ds(HALF, cols), :]
        return pltpu.make_async_remote_copy(
            src_ref=theirs,
            dst_ref=theirs,
            send_sem=surf_send.at[j - 1],
            recv_sem=surf_recv.at[j - 1],
            device_id=(gx, lax.rem(gz + j, n_gz)),
            device_id_type=MESH,
        )

    for j in range(1, n_gz):
        surf_copy(j).start()

    for c in range(CHUNKS):
        for copy in chunk_loads[c][: 2 * bands]:
            copy.wait()

    def mobility(logk):
        return (0.5 * STEP_SIZE) * jnp.exp(logk)

    def pack(i):
        z0 = pl.multiple_of(i * 16, 16)
        r0 = pl.multiple_of(i * 16 * cols, 16 * cols)
        for s in range(2):
            line = pl.ds(r0 + s * (cols - 1), 16, stride=cols)
            fields = (get(adj, line), mobility(get(mob, line)))
            near_adj[0, s, pl.ds(z0, 16), :] = fields[0]
            near_mob[s, pl.ds(z0, 16), :] = fields[1]
            for k, field in enumerate(fields):
                send_halo[s, pl.ds(k * depth + z0, 16), :] = field.astype(jnp.bfloat16)

    every(0, depth // 16, 1, pack)

    def swap(sent, arrived, send_sem, recv_sem):
        def leave(s):
            return pltpu.make_async_remote_copy(
                src_ref=sent.at[s],
                dst_ref=arrived.at[1 - s],
                send_sem=send_sem.at[s],
                recv_sem=recv_sem.at[1 - s],
                device_id=(beside[s], gz),
                device_id_type=MESH,
            )

        def come(s):
            return pltpu.make_async_remote_copy(
                src_ref=sent.at[1 - s],
                dst_ref=arrived.at[s],
                send_sem=send_sem.at[1 - s],
                recv_sem=recv_sem.at[s],
                device_id=(beside[s], gz),
                device_id_type=MESH,
            )

        return leave, come

    top_leave, top_come = swap(send_top, recv_top, top_send, top_recv)
    halo_leave, halo_come = swap(send_halo, recv_halo, halo_send, halo_recv)
    prs_leave, prs_come = swap(send_prs, recv_prs, prs_send, prs_recv)
    mid_leave, mid_come = swap(send_mid, recv_mid, mid_send, mid_recv)

    for s in range(2):

        @pl.when(has[s])
        def _():
            top_leave(s).start()
            halo_leave(s).start()

    small[4].wait()
    kpad[...] = jnp.zeros(kpad.shape, jnp.float32)
    kpad[:, 0 : SIDE * SIDE] = kernel_ref[...]
    for x in range(8):
        put(toep, pl.ds(x, depth, stride=8), pltpu.roll(kpad[...], SIDE * x, 1))
    tail = shifted.shape[1] - (cols + 2 * HALF) * SIDE
    put(shifted, pl.ds((cols + 2 * HALF) * SIDE, tail), jnp.zeros((tail, rows), jnp.float32))

    def halve(i):
        tile = pl.ds(pl.multiple_of(i * 64, 64), 64)
        piece = get(toep, tile)
        hi = piece.astype(jnp.bfloat16)
        toep_hi[tile, :] = hi
        toep_lo[tile, :] = (piece - hi.astype(jnp.float32)).astype(jnp.bfloat16)

    every(0, depth * 8 // 64, 1, halve)

    z_base = gz * depth

    def next_x(ref, at):
        return get(ref, pl.ds(at + 1, cols))

    def next_y(value):
        return pltpu.roll(value, rows - 1, 1)

    def narrow_roll(value, by):
        return pltpu.roll(value.astype(jnp.bfloat16), by, 1).astype(jnp.float32)

    def lower(at):
        return pl.ds(pl.multiple_of(at + 8, 8), cols)

    def lateral(level, a, a_next, at, face_x, face_y):
        put(fx, lower(at), face_x * (a_next - a))
        dy = next_y(a) - a
        steps_y[level, pl.ds(at, cols), :] = dy
        fy = face_y * dy
        part_exp[pl.ds(at, cols), :] = a + (fy - narrow_roll(fy, 1))

    def level_first(i, decay):
        z = depth - 1 - i
        at = pl.multiple_of(z * cols, cols)
        here = pl.ds(at, cols)
        zf = (z_base + z).astype(jnp.float32)
        m = mobility(get(mob, here))
        face_x = jnp.where(tops[1] <= zf, m + mobility(next_x(mob, at)), 0.0)
        face_y = jnp.where(tops[2] <= zf, m + narrow_roll(m, rows - 1), 0.0)
        tx[here, :] = face_x
        ty[here, :] = face_y
        lateral(0, get(adj, here), next_x(adj, at), at, face_x, face_y)
        r = 1.0 / (1.0 + ver[here, :].astype(jnp.float32))
        live = tops[0] <= zf
        rec[here, :] = jnp.where(live, r, 0.0)
        f = jnp.where(live, 1.0 - r, 0.0)
        fac[here, :] = f
        decay = f * decay
        put(dec, here, decay)
        return decay

    decay = jnp.ones((cols, rows), jnp.float32)
    for c in range(CHUNKS):
        chunk_loads[c][2 * bands].wait()
    decay = lax.fori_loop(0, depth // 2, level_first, decay, unroll=UNROLL)

    def edge_copy(s):
        first = HALF + s * (cols - HALF)
        return pltpu.make_async_remote_copy(
            src_ref=surf.at[:, pl.ds(first, HALF), :],
            dst_ref=surf.at[:, pl.ds((1 - s) * (HALF + cols), HALF), :],
            send_sem=edge_send.at[s],
            recv_sem=edge_recv.at[1 - s],
            device_id=(beside[s], gz),
            device_id_type=MESH,
        )

    def edge_arrival(s):
        first = HALF + (1 - s) * (cols - HALF)
        return pltpu.make_async_remote_copy(
            src_ref=surf.at[:, pl.ds(first, HALF), :],
            dst_ref=surf.at[:, pl.ds(s * (HALF + cols), HALF), :],
            send_sem=edge_send.at[1 - s],
            recv_sem=edge_recv.at[s],
            device_id=(beside[s], gz),
            device_id_type=MESH,
        )

    for j in range(1, n_gz):
        surf_arrival(j).wait_recv()
    for s in range(2):

        @pl.when(has[s])
        def _():
            edge_copy(s).start()

    lax.fori_loop(depth // 2, depth, level_first, decay, unroll=UNROLL)

    def side_steps(level, s, i):
        z0 = pl.multiple_of(i * 16, 16)
        part = pl.ds(z0, 16)
        x = s * (cols - 1)
        zf = (z_base + z0 + lax.broadcasted_iota(jnp.int32, (16, rows), 0)).astype(jnp.float32)
        far = (recv_halo if level == 0 else recv_mid)[s, part, :].astype(jnp.float32)
        face = jnp.maximum(tops[0, x : x + 1, :], recv_top[s, 0:1, :])
        return part, jnp.where(face <= zf, far - near_adj[level, s, part, :], 0.0)

    def edges(level):
        def step(i):
            for s in range(2):
                part, d = side_steps(level, s, i)
                far_m = recv_halo[s, pl.ds(pl.multiple_of(depth + i * 16, 16), 16), :]
                put(edge_flux.at[s], part, (near_mob[s, part, :] + far_m.astype(jnp.float32)) * d)

        every(0, depth // 16, 1, step)

    def edge_terms():
        def step(i):
            for s in range(2):
                total = None
                for level in range(2):
                    part, d = side_steps(level, s, i)
                    p_part = pl.ds(pl.multiple_of(level * depth + i * 16, 16), 16)
                    far_p = recv_prs[s, p_part, :].astype(jnp.float32)
                    term = d * (far_p - send_prs[s, p_part, :].astype(jnp.float32))
                    total = term if total is None else total + term
                put(edge_term.at[s], part, total)

        every(0, depth // 16, 1, step)

    def face_terms(level, add):
        state = (adj, mid)[level]

        def step(z):
            at = pl.multiple_of(z * cols, cols)
            here = pl.ds(at, cols)
            zf = (z_base + z).astype(jnp.float32)
            p = prs[pl.ds(pl.multiple_of(level * cells + at, cols), cols), :].astype(jnp.float32)
            a = get(state, here)
            dx = jnp.where(tops[1] <= zf, next_x(state, at) - a, 0.0)
            dy = jnp.where(tops[2] <= zf, steps_y[level, here, :], 0.0)
            term_x = dx * (pltpu.roll(p, cols - 1, 0) - p)
            term_y = dy * (next_y(p) - p)
            if add:
                term_x = term_x + get(gx_sum, lower(at))
                term_y = term_y + gy_sum[here, :]
            put(gx_sum, lower(at), term_x)
            gy_sum[here, :] = term_y

        every(0, depth, UNROLL, step)

    def send_pressures():
        z_of = lax.broadcasted_iota(jnp.int32, (32, 256), 0)
        k_of = lax.broadcasted_iota(jnp.int32, (32, 256), 1)
        pick = (k_of == jnp.where(z_of < 16, z_of * cols, z_of * cols - 15 * cols - 1)).astype(
            jnp.bfloat16
        )

        def step(i):
            block = prs[pl.ds(pl.multiple_of(i * 256, 256), 256), :]
            lines = jnp.dot(pick, block, preferred_element_type=jnp.float32).astype(jnp.bfloat16)
            part = pl.ds(pl.multiple_of(i * 16, 16), 16)
            send_prs[0, part, :] = lines[:16, :]
            send_prs[1, part, :] = lines[16:, :]

        every(0, 2 * depth // 16, 1, step)
        for s in range(2):

            @pl.when(has[s])
            def _():
                prs_leave(s).start()

    for s in range(2):

        @pl.when(has[s])
        def _():
            edge_arrival(s).wait_recv()

    surface = jnp.concatenate([surf[g] for g in range(n_gz)], axis=1)
    wide_y = lax.broadcasted_iota(jnp.int32, surface.shape, 1)
    for b in range(SIDE):
        off = b - HALF
        turned = surface if off == 0 else pltpu.roll(surface, (-off) % rows, 1)
        if off > 0:
            turned = jnp.where(wide_y < rows - off, turned, 0.0)
        if off < 0:
            turned = jnp.where(wide_y >= -off, turned, 0.0)
        put(shifted, pl.ds(b, cols + 2 * HALF, stride=SIDE), turned)
    for h in range(2):
        for q in range(4):
            piece = get(shifted, pl.ds(h * 8 * SIDE + q * 128, 128))
            hi = piece.astype(jnp.bfloat16)
            rhs_hi[h, pl.ds(q * 128, 128), :] = hi
            rhs_lo[h, pl.ds(q * 128, 128), :] = (piece - hi.astype(jnp.float32)).astype(
                jnp.bfloat16
            )

    def product(i):
        tile = pl.ds(pl.multiple_of(i * 256, 256), 256)
        for h in range(2):
            src[h, tile, :] = (
                jnp.dot(toep_hi[tile, :], rhs_hi[h], preferred_element_type=jnp.float32)
                + jnp.dot(toep_hi[tile, :], rhs_lo[h], preferred_element_type=jnp.float32)
                + jnp.dot(toep_lo[tile, :], rhs_hi[h], preferred_element_type=jnp.float32)
            )

    every(0, depth * 8 // 256, 1, product)

    row_id = lax.broadcasted_iota(jnp.int32, (8, rows), 0)

    def edge_rows(ref, z, h):
        line = get(ref.at[h], pl.ds(z, 1))
        return jnp.where(row_id == 7 * h, line, 0.0)

    def chain(i, below):
        z = depth - 1 - i
        eight = pl.ds(pl.multiple_of(z * 8, 8), 8)
        solved = []
        for h in range(2):
            at = pl.multiple_of(z * cols + 8 * h, 8)
            part = pl.ds(at, 8)
            across = get(fx, pl.ds(pl.multiple_of(at + 8, 8), 8)) - get(fx, pl.ds(at + 7, 8))
            e = (part_exp[part, :] + across) + (src[h, eight, :] + edge_rows(edge_flux, z, h))
            v = fac[part, :] * below[h] + rec[part, :] * e
            put(low, part, v)
            solved.append(v)
        return tuple(solved)

    for s in range(2):

        @pl.when(has[s])
        def _():
            top_come(s).wait_recv()
            halo_come(s).wait_recv()

    edges(0)
    nothing = (jnp.zeros((8, rows), jnp.float32),) * 2
    lax.fori_loop(0, depth, chain, nothing, unroll=4)

    def inc_copy(level, to):
        return pltpu.make_async_remote_copy(
            src_ref=send_inc.at[level],
            dst_ref=recv_inc.at[level],
            send_sem=inc_send.at[level],
            recv_sem=inc_recv.at[level],
            device_id=(gx, to),
            device_id_type=MESH,
        )

    def relay(level):
        @pl.when(gz < n_gz - 1)
        def _():
            inc_copy(level, gz + 1).wait_recv()

        @pl.when(gz > 0)
        def _():
            first = pl.ds(0, cols)
            send_inc[level] = get(low, first) + get(dec, first) * recv_inc[level]
            inc_copy(level, gz - 1).start()

    load_prs.wait()
    early = gz < n_gz // 2

    @pl.when(early)
    def _():
        send_pressures()
        face_terms(0, False)

    relay(0)

    def pack_mid(i):
        z0 = pl.multiple_of(i * 16, 16)
        r0 = pl.multiple_of(i * 16 * cols, 16 * cols)
        for s in range(2):
            x = s * (cols - 1)
            line = pl.ds(r0 + x, 16, stride=cols)
            value = get(low, line) + get(dec, line) * recv_inc[0, x : x + 1, :]
            near_adj[1, s, pl.ds(z0, 16), :] = value
            send_mid[s, pl.ds(z0, 16), :] = value.astype(jnp.bfloat16)

    every(0, depth // 16, 2, pack_mid)

    for s in range(2):

        @pl.when(has[s])
        def _():
            mid_leave(s).start()

    below_next = pltpu.roll(recv_inc[0], cols - 1, 0)

    def level_second(z):
        at = pl.multiple_of(z * cols, cols)
        here = pl.ds(at, cols)
        a = get(low, here) + get(dec, here) * recv_inc[0]
        a_next = next_x(low, at) + next_x(dec, at) * below_next
        put(mid, here, a)
        lateral(1, a, a_next, at, tx[here, :], ty[here, :])

    every(0, depth, UNROLL, level_second)

    @pl.when(early)
    def _():
        face_terms(1, True)

    @pl.when(jnp.logical_not(early))
    def _():
        send_pressures()
        face_terms(1, False)

    for s in range(2):

        @pl.when(has[s])
        def _():
            mid_come(s).wait_recv()

    edges(1)
    lax.fori_loop(0, depth, chain, nothing, unroll=4)
    relay(1)

    @pl.when(jnp.logical_not(early))
    def _():
        face_terms(0, True)

    for s in range(2):

        @pl.when(has[s])
        def _():
            prs_come(s).wait_recv()

    edge_terms()

    def finish(z):
        at = pl.multiple_of(z * cols, cols)
        here = pl.ds(at, cols)
        out_ref[here, :] = get(low, here) + get(dec, here) * recv_inc[1]
        along = gy_sum[here, :]
        along = along + pltpu.roll(along, 1, 1)
        across = get(gx_sum, lower(at)) + get(gx_sum, pl.ds(at + 7, cols))
        ends = jnp.concatenate([edge_rows(edge_term, z, h) for h in range(2)], axis=0)
        grad_ref[here, :] = mobility(get(mob, here)) * ((along + across) + ends)

    every(0, depth, 4, finish)

    for j in range(1, n_gz):
        surf_copy(j).wait_send()
    for s in range(2):

        @pl.when(has[s])
        def _():
            top_leave(s).wait_send()
            halo_leave(s).wait_send()
            prs_leave(s).wait_send()
            edge_copy(s).wait_send()
            mid_leave(s).wait_send()

    @pl.when(gz > 0)
    def _():
        inc_copy(0, gz - 1).wait_send()
        inc_copy(1, gz - 1).wait_send()


def on_device(
    n_gx,
    n_gz,
    residual,
    whitening,
    kernel,
    adjoint_end,
    pressure,
    log_permeability,
    vertical,
    top_layer,
    well_columns,
):
    depth, cols, rows = adjoint_end.shape
    cells = depth * cols
    f32, b16 = jnp.float32, jnp.bfloat16
    lanes = rows // LANES
    vmem = pltpu.VMEM
    field = vmem((cells, rows), f32)
    banded = vmem((lanes, cells + 8, LANES), f32)
    dma = pltpu.SemaphoreType.DMA
    wide = cols + 2 * HALF
    hbm = pl.BlockSpec(memory_space=pl.ANY)
    adjoint_start, gradient = pl.pallas_call(
        functools.partial(window_kernel, n_gx, n_gz, depth, cols, rows),
        out_shape=(vmem((cells, rows), f32),) * 2,
        in_specs=[hbm] * 9,
        out_specs=(pl.BlockSpec(memory_space=vmem),) * 2,
        scratch_shapes=[
            vmem(residual.shape, f32),
            vmem(whitening.shape, f32),
            vmem(kernel.shape, f32),
            vmem(top_layer.shape, jnp.int32),
            pltpu.SMEM(well_columns.shape, jnp.int32),
            banded,
            vmem((2 * cells, rows), b16),
            banded,
            vmem((cells, rows), b16),
            field,
            field,
            banded,
            banded,
            field,
            field,
            vmem((2, cells, rows), f32),
            field,
            field,
            banded,
            banded,
            banded,
            vmem((2, depth * 8, rows), f32),
            vmem((n_gz, wide, rows // n_gz), f32),
            vmem((lanes, 8 * SIDE + 512, LANES), f32),
            vmem((2, 512, rows), b16),
            vmem((2, 512, rows), b16),
            vmem((depth, 512), f32),
            vmem((4, depth * 8, LANES), f32),
            vmem((depth * 8, 512), b16),
            vmem((depth * 8, 512), b16),
            vmem((3, cols, rows), f32),
            vmem((2, 2, depth, rows), f32),
            vmem((2, depth, rows), f32),
            vmem((2, lanes, depth, LANES), f32),
            vmem((2, lanes, depth, LANES), f32),
            vmem((2, 2 * depth, rows), b16),
            vmem((2, 2 * depth, rows), b16),
            vmem((2, 2 * depth, rows), b16),
            vmem((2, 2 * depth, rows), b16),
            vmem((2, 8, rows), f32),
            vmem((2, 8, rows), f32),
            vmem((2, depth, rows), b16),
            vmem((2, depth, rows), b16),
            vmem((2, cols, rows), f32),
            vmem((2, cols, rows), f32),
            dma((6,)),
            dma((CHUNKS, 1 + 2 * lanes)),
            dma((n_gz - 1,)),
            dma((n_gz - 1,)),
        ]
        + [dma((2,))] * 12,
        compiler_params=pltpu.CompilerParams(
            collective_id=0, has_side_effects=True, vmem_limit_bytes=56 * 1024 * 1024
        ),
    )(
        residual,
        whitening,
        kernel,
        top_layer,
        well_columns,
        adjoint_end.reshape(cells, rows),
        pressure.reshape(2 * cells, rows),
        log_permeability.reshape(cells, rows),
        vertical.reshape(cells, rows),
    )
    shape = (depth, cols, rows)
    return adjoint_start.reshape(shape), gradient.reshape(shape)


def solution(mesh):
    in_specs = (
        P("gx", "gz"),
        P("gx", "gz"),
        P("gz", None),
        P("gz", "gx", None),
        P(None, "gz", "gx", None),
        P("gz", "gx", None),
        P("gz", "gx", None),
        P("gx", None),
        P(),
    )
    out_specs = (P("gz", "gx", None), P("gz", "gx", None))
    return jax.shard_map(
        functools.partial(on_device, mesh.shape["gx"], mesh.shape["gz"]),
        mesh=mesh,
        in_specs=in_specs,
        out_specs=out_specs,
        check_vma=False,
    )
```

```python
import functools

import jax
import jax.numpy as jnp
from jax import lax
from jax.experimental import pallas as pl
from jax.experimental.pallas import tpu as pltpu
from jax.sharding import PartitionSpec as P

STEP_SIZE = 0.1
HALF = 8
SIDE = 17
FAR = 1e6
MESH = pl.DeviceIdType.MESH
CHUNKS = 2
UNROLL = 4
STORES = 4
SPLIT = 48
LANES = 128


def get(ref, at):
    return jnp.concatenate([ref[q, at, :] for q in range(ref.shape[0])], axis=1)


def put(ref, at, value):
    for q in range(ref.shape[0]):
        ref[q, at, :] = value[:, q * LANES : (q + 1) * LANES]


def every(low, high, unroll, body):
    def step(i, carry):
        body(i)
        return carry

    lax.fori_loop(low, high, step, 0, unroll=unroll)


def edge_rows(ref, z, h, rows):
    row_id = lax.broadcasted_iota(jnp.int32, (8, rows), 0)
    return jnp.where(row_id == 7 * h, get(ref.at[h], pl.ds(z, 1)), 0.0)


def finish_kernel(
    n_gx,
    depth,
    cols,
    rows,
    low,
    dec,
    inc_ref,
    gx_sum,
    gy_sum,
    mob,
    edge_term,
    top_ref,
    out_hbm,
    grad_hbm,
    out,
    grad,
    sem,
):
    z_base = lax.axis_index("gz") * depth
    chunk = depth // STORES

    def finish(z):
        at = pl.multiple_of(z * cols, cols)
        here = pl.ds(at, cols)
        live = top_ref[...] <= (z_base + z).astype(jnp.float32)
        out[here, :] = jnp.where(live, get(low, here) + get(dec, here) * inc_ref[...], 0.0)
        across = get(gx_sum, pl.ds(pl.multiple_of(at + 8, 8), cols)) + get(
            gx_sum, pl.ds(at + 7, cols)
        )
        ends = jnp.concatenate([edge_rows(edge_term, z, h, rows) for h in range(2)], axis=0)
        grad[here, :] = get(mob, here) * ((gy_sum[here, :] + across) + ends)

    def stores(c):
        part = pl.ds(c * chunk * cols, chunk * cols)
        return [
            pltpu.make_async_copy(a.at[part], b.at[part], sem.at[c, i])
            for i, (a, b) in enumerate(((out, out_hbm), (grad, grad_hbm)))
        ]

    pending = []
    for c in range(STORES):
        every(c * chunk, (c + 1) * chunk, 4, finish)
        copies = stores(c)
        for copy in copies:
            copy.start()
        pending += copies
    for copy in pending:
        copy.wait()


def window_kernel(
    n_gx,
    n_gz,
    depth,
    cols,
    rows,
    residual_hbm,
    whitening_hbm,
    kernel_hbm,
    top_hbm,
    wells_hbm,
    adjoint_hbm,
    pressure_hbm,
    logk_hbm,
    vertical_hbm,
    low,
    dec,
    inc_ref,
    gx_sum,
    gy_sum,
    mob,
    edge_term,
    top_out,
    residual_ref,
    whitening_ref,
    kernel_ref,
    top_ref,
    wells_ref,
    adj,
    prs,
    logk,
    ver,
    tx,
    ty,
    face_y,
    fx,
    fy_narrow,
    flux_y,
    steps_y,
    gx_part,
    gy_part,
    step_x,
    step_y,
    rec,
    mid,
    src,
    surf,
    shifted,
    rhs_hi,
    rhs_lo,
    kpad,
    toep,
    toep_hi,
    toep_lo,
    tops,
    near_adj,
    near_mob,
    edge_flux,
    pair_sum,
    pair_step,
    send_halo,
    recv_halo,
    send_prs,
    recv_prs,
    send_top,
    recv_top,
    send_mid,
    recv_mid,
    send_inc,
    recv_inc,
    small_sem,
    load_sem,
    surf_send,
    surf_recv,
    edge_send,
    edge_recv,
    halo_send,
    halo_recv,
    prs_send,
    prs_recv,
    top_send,
    top_recv,
    mid_send,
    mid_recv,
    inc_send,
    inc_recv,
):
    gx = lax.axis_index("gx")
    gz = lax.axis_index("gz")
    layers = depth // CHUNKS
    span = layers * cols
    cells = depth * cols
    bands = rows // LANES
    has = (gx > 0, gx < n_gx - 1)
    beside = (gx - 1, gx + 1)

    barrier = pltpu.get_barrier_semaphore()
    for j in range(1, n_gz):
        pl.semaphore_signal(
            barrier, inc=1, device_id=(gx, lax.rem(gz + j, n_gz)), device_id_type=MESH
        )
    for s in range(2):

        @pl.when(has[s])
        def _():
            pl.semaphore_signal(barrier, inc=1, device_id=(beside[s], gz), device_id_type=MESH)

    small = [
        pltpu.make_async_copy(a, b, small_sem.at[i])
        for i, (a, b) in enumerate(
            (
                (residual_hbm, residual_ref),
                (whitening_hbm, whitening_ref),
                (top_hbm, top_ref),
                (wells_hbm, wells_ref),
                (kernel_hbm, kernel_ref),
            )
        )
    ]
    for copy in small:
        copy.start()

    def loads(c):
        at = c * span
        here = pl.ds(at, span)
        pairs = []
        for q in range(bands):
            lane = pl.ds(q * LANES, LANES)
            pairs.append((logk_hbm.at[here, lane], logk.at[q, here]))
            pairs.append((adjoint_hbm.at[here, lane], adj.at[q, here]))
        pairs.append((vertical_hbm.at[here], ver.at[here]))
        return [
            pltpu.make_async_copy(a, b, load_sem.at[c, i]) for i, (a, b) in enumerate(pairs)
        ]

    chunk_loads = [loads(c) for c in range(CHUNKS)]
    for copies in reversed(chunk_loads):
        for copy in copies[: 2 * bands]:
            copy.start()
    for copies in reversed(chunk_loads):
        copies[2 * bands].start()
    load_prs = pltpu.make_async_copy(pressure_hbm, prs, small_sem.at[5])
    load_prs.start()

    for s in range(2):

        @pl.when(jnp.logical_not(has[s]))
        def _():
            first = s * (HALF + cols)
            surf[:, first : first + HALF, :] = jnp.zeros((n_gz, HALF, rows // n_gz), jnp.float32)
            recv_halo[s] = jnp.zeros(recv_halo.shape[1:], recv_halo.dtype)
            recv_top[s] = jnp.full(recv_top.shape[1:], FAR, jnp.float32)
            recv_mid[s] = jnp.zeros(recv_mid.shape[1:], recv_mid.dtype)
            recv_prs[s] = jnp.zeros(recv_prs.shape[1:], recv_prs.dtype)

    @pl.when(gz == n_gz - 1)
    def _():
        recv_inc[...] = jnp.zeros(recv_inc.shape, jnp.float32)

    blank = jnp.zeros((8, rows), jnp.float32)
    after = pl.ds(cells, 8)
    for ref in (mob, adj, low, dec, mid, logk):
        put(ref, after, blank)
    for ref in (fx, gx_sum, gx_part):
        put(ref, pl.ds(0, 8), blank)

    small[0].wait()
    small[1].wait()
    strip = surf.at[gz]
    strip[HALF : HALF + cols, :] = residual_ref[...] * whitening_ref[...]

    small[2].wait()
    small[3].wait()
    cell = (
        (gx * cols + lax.broadcasted_iota(jnp.int32, (cols, rows), 0)) * rows
        + lax.broadcasted_iota(jnp.int32, (cols, rows), 1)
    )

    def drill(i, top):
        return jnp.where(cell == wells_ref[i], FAR, top)

    top = lax.fori_loop(
        0, wells_ref.shape[0], drill, top_ref[...].astype(jnp.float32), unroll=8
    )
    x_id = lax.broadcasted_iota(jnp.int32, (cols, rows), 0)
    y_id = lax.broadcasted_iota(jnp.int32, (cols, rows), 1)
    tops[0] = top
    top_out[...] = top
    tops[1] = jnp.where(x_id == cols - 1, FAR, jnp.maximum(top, pltpu.roll(top, cols - 1, 0)))
    tops[2] = jnp.where(y_id == rows - 1, FAR, jnp.maximum(top, pltpu.roll(top, rows - 1, 1)))
    send_top[0] = jnp.broadcast_to(top[0:1, :], (8, rows))
    send_top[1] = jnp.broadcast_to(top[cols - 1 : cols, :], (8, rows))

    small[4].wait()
    kpad[...] = jnp.zeros(kpad.shape, jnp.float32)
    kpad[:, 0 : SIDE * SIDE] = kernel_ref[...]
    for x in range(8):
        put(toep, pl.ds(x, depth, stride=8), pltpu.roll(kpad[...], SIDE * x, 1))
    tail = shifted.shape[1] - (cols + 2 * HALF) * SIDE
    put(shifted, pl.ds((cols + 2 * HALF) * SIDE, tail), jnp.zeros((tail, rows), jnp.float32))

    def halve(i):
        tile = pl.ds(pl.multiple_of(i * 64, 64), 64)
        piece = get(toep, tile)
        hi = piece.astype(jnp.bfloat16)
        toep_hi[tile, :] = hi
        toep_lo[tile, :] = (piece - hi.astype(jnp.float32)).astype(jnp.bfloat16)

    every(0, depth * 8 // 64, 1, halve)

    tile = rows // 2
    k_id = lax.broadcasted_iota(jnp.int32, (rows, tile), 0)
    n_id = lax.broadcasted_iota(jnp.int32, (rows, tile), 1)
    same, nearby = k_id == n_id, k_id == n_id + 1
    pair_sum[...] = jnp.where(same, 1.0, jnp.where(nearby, 1.0, 0.0)).astype(jnp.bfloat16)
    same, nearby = k_id == n_id + tile, k_id + 1 == n_id + tile
    pair_step[...] = jnp.where(same, 1.0, jnp.where(nearby, -1.0, 0.0)).astype(jnp.bfloat16)

    strips_beside = jnp.where(has[0], 1, 0) + jnp.where(has[1], 1, 0)
    pl.semaphore_wait(barrier, n_gz - 1 + strips_beside)

    def surf_copy(j):
        mine = surf.at[gz, pl.ds(HALF, cols), :]
        return pltpu.make_async_remote_copy(
            src_ref=mine,
            dst_ref=mine,
            send_sem=surf_send.at[j - 1],
            recv_sem=surf_recv.at[j - 1],
            device_id=(gx, lax.rem(gz + j, n_gz)),
            device_id_type=MESH,
        )

    def surf_arrival(j):
        theirs = surf.at[lax.rem(gz + n_gz - j, n_gz), pl.ds(HALF, cols), :]
        return pltpu.make_async_remote_copy(
            src_ref=theirs,
            dst_ref=theirs,
            send_sem=surf_send.at[j - 1],
            recv_sem=surf_recv.at[j - 1],
            device_id=(gx, lax.rem(gz + j, n_gz)),
            device_id_type=MESH,
        )

    for j in range(1, n_gz):
        surf_copy(j).start()

    block = 16 * cols

    def product_of(lhs, rhs):
        return jnp.dot(lhs, rhs, preferred_element_type=jnp.float32)

    def mobilities(i):
        at = pl.ds(pl.multiple_of(i * block, block), block)
        m = (0.5 * STEP_SIZE) * jnp.exp(get(logk, at))
        put(mob, at, m)
        m = m.astype(jnp.bfloat16)
        face_y[at, :tile] = product_of(m, pair_sum[...])
        face_y[at, tile:] = product_of(m[:, tile:], pair_sum[:tile, :])

    def flux_steps(i):
        at = pl.ds(pl.multiple_of(i * block, block), block)
        f = fy_narrow[at, :]
        flux_y[at, :tile] = product_of(f[:, :tile], pair_step[tile:, :])
        flux_y[at, tile:] = product_of(f, pair_step[...])

    for c in reversed(range(CHUNKS)):
        for copy in chunk_loads[c][: 2 * bands]:
            copy.wait()
        every(c * span // block, (c + 1) * span // block, 2, mobilities)

    def pack(i):
        z0 = pl.multiple_of(i * 16, 16)
        r0 = pl.multiple_of(i * 16 * cols, 16 * cols)
        for s in range(2):
            line = pl.ds(r0 + s * (cols - 1), 16, stride=cols)
            fields = (get(adj, line), get(mob, line))
            near_adj[0, s, pl.ds(z0, 16), :] = fields[0]
            near_mob[s, pl.ds(z0, 16), :] = fields[1]
            for k, field in enumerate(fields):
                send_halo[s, pl.ds(k * depth + z0, 16), :] = field.astype(jnp.bfloat16)

    every(0, depth // 16, 1, pack)

    def swap(sent, arrived, send_sem, recv_sem):
        def leave(s):
            return pltpu.make_async_remote_copy(
                src_ref=sent.at[s],
                dst_ref=arrived.at[1 - s],
                send_sem=send_sem.at[s],
                recv_sem=recv_sem.at[1 - s],
                device_id=(beside[s], gz),
                device_id_type=MESH,
            )

        def come(s):
            return pltpu.make_async_remote_copy(
                src_ref=sent.at[1 - s],
                dst_ref=arrived.at[s],
                send_sem=send_sem.at[1 - s],
                recv_sem=recv_sem.at[s],
                device_id=(beside[s], gz),
                device_id_type=MESH,
            )

        return leave, come

    top_leave, top_come = swap(send_top, recv_top, top_send, top_recv)
    halo_leave, halo_come = swap(send_halo, recv_halo, halo_send, halo_recv)
    prs_leave, prs_come = swap(send_prs, recv_prs, prs_send, prs_recv)
    mid_leave, mid_come = swap(send_mid, recv_mid, mid_send, mid_recv)

    for s in range(2):

        @pl.when(has[s])
        def _():
            top_leave(s).start()
            halo_leave(s).start()

    z_base = gz * depth

    def next_x(ref, at):
        return get(ref, pl.ds(at + 1, cols))

    def next_y(value):
        return pltpu.roll(value, rows - 1, 1)

    def lower(at):
        return pl.ds(pl.multiple_of(at + 8, 8), cols)

    def lateral(level, a, a_next, at, open_x, open_y):
        here = pl.ds(at, cols)
        put(fx, lower(at), open_x * (a_next - a))
        dy = next_y(a) - a
        steps_y[level, here, :] = dy
        fy_narrow[here, :] = (open_y * dy).astype(jnp.bfloat16)

    def level_first(i, decay):
        z = depth - 1 - i
        at = pl.multiple_of(z * cols, cols)
        here = pl.ds(at, cols)
        zf = (z_base + z).astype(jnp.float32)
        open_x = jnp.where(tops[1] <= zf, get(mob, here) + next_x(mob, at), 0.0)
        open_y = jnp.where(tops[2] <= zf, face_y[here, :], 0.0)
        tx[here, :] = open_x
        ty[here, :] = open_y
        lateral(0, get(adj, here), next_x(adj, at), at, open_x, open_y)
        r = jnp.where(tops[0] <= zf, 1.0 / (1.0 + ver[here, :].astype(jnp.float32)), 0.0)
        rec[here, :] = r
        decay = decay - r * decay
        put(dec, here, decay)
        return decay

    decay = jnp.ones((cols, rows), jnp.float32)
    for c in range(CHUNKS):
        chunk_loads[c][2 * bands].wait()
    decay = lax.fori_loop(0, SPLIT, level_first, decay, unroll=UNROLL)

    def edge_copy(s):
        first = HALF + s * (cols - HALF)
        return pltpu.make_async_remote_copy(
            src_ref=surf.at[:, pl.ds(first, HALF), :],
            dst_ref=surf.at[:, pl.ds((1 - s) * (HALF + cols), HALF), :],
            send_sem=edge_send.at[s],
            recv_sem=edge_recv.at[1 - s],
            device_id=(beside[s], gz),
            device_id_type=MESH,
        )

    def edge_arrival(s):
        first = HALF + (1 - s) * (cols - HALF)
        return pltpu.make_async_remote_copy(
            src_ref=surf.at[:, pl.ds(first, HALF), :],
            dst_ref=surf.at[:, pl.ds(s * (HALF + cols), HALF), :],
            send_sem=edge_send.at[1 - s],
            recv_sem=edge_recv.at[s],
            device_id=(beside[s], gz),
            device_id_type=MESH,
        )

    for j in range(1, n_gz):
        surf_arrival(j).wait_recv()
    for s in range(2):

        @pl.when(has[s])
        def _():
            edge_copy(s).start()

    lax.fori_loop(SPLIT, depth, level_first, decay, unroll=UNROLL)
    every(0, cells // block, 4, flux_steps)

    def side_steps(level, s, i):
        z0 = pl.multiple_of(i * 16, 16)
        part = pl.ds(z0, 16)
        x = s * (cols - 1)
        zf = (z_base + z0 + lax.broadcasted_iota(jnp.int32, (16, rows), 0)).astype(jnp.float32)
        far = (recv_halo if level == 0 else recv_mid)[s, part, :].astype(jnp.float32)
        face = jnp.maximum(tops[0, x : x + 1, :], recv_top[s, 0:1, :])
        return part, jnp.where(face <= zf, far - near_adj[level, s, part, :], 0.0)

    def edges(level):
        def step(i):
            for s in range(2):
                part, d = side_steps(level, s, i)
                far_m = recv_halo[s, pl.ds(pl.multiple_of(depth + i * 16, 16), 16), :]
                put(edge_flux.at[s], part, (near_mob[s, part, :] + far_m.astype(jnp.float32)) * d)

        every(0, depth // 16, 1, step)

    def edge_terms():
        def step(i):
            for s in range(2):
                total = None
                for level in range(2):
                    part, d = side_steps(level, s, i)
                    p_part = pl.ds(pl.multiple_of(level * depth + i * 16, 16), 16)
                    far_p = recv_prs[s, p_part, :].astype(jnp.float32)
                    term = d * (far_p - send_prs[s, p_part, :].astype(jnp.float32))
                    total = term if total is None else total + term
                put(edge_term.at[s], part, total)

        every(0, depth // 16, 1, step)

    def pressure_steps(level, z, at):
        zf = (z_base + z).astype(jnp.float32)
        p = prs[pl.ds(pl.multiple_of(level * cells + at, cols), cols), :].astype(jnp.float32)
        across = jnp.where(tops[1] <= zf, pltpu.roll(p, cols - 1, 0) - p, 0.0)
        return across, jnp.where(tops[2] <= zf, next_y(p) - p, 0.0)

    def prepare_terms(z):
        at = pl.multiple_of(z * cols, cols)
        across, along = pressure_steps(1, z, at)
        step_x[pl.ds(at, cols), :] = across
        step_y[pl.ds(at, cols), :] = along

    def face_terms(level, add, ready):
        state = (adj, mid)[level]

        def step(z):
            at = pl.multiple_of(z * cols, cols)
            here = pl.ds(at, cols)
            if ready:
                across, along = step_x[here, :], step_y[here, :]
            else:
                across, along = pressure_steps(level, z, at)
            term_x = (next_x(state, at) - get(state, here)) * across
            term_y = steps_y[level, here, :] * along
            if add:
                term_x = term_x + get(gx_part, lower(at))
                term_y = term_y + gy_part[here, :]
                gy_sum[here, :] = term_y + pltpu.roll(term_y, 1, 1)
            else:
                gy_part[here, :] = term_y
            put(gx_sum if add else gx_part, lower(at), term_x)

        every(0, depth, UNROLL, step)

    def pack_pressures():
        z_of = lax.broadcasted_iota(jnp.int32, (32, 256), 0)
        k_of = lax.broadcasted_iota(jnp.int32, (32, 256), 1)
        pick = (k_of == jnp.where(z_of < 16, z_of * cols, z_of * cols - 15 * cols - 1)).astype(
            jnp.bfloat16
        )

        def step(i):
            block = prs[pl.ds(pl.multiple_of(i * 256, 256), 256), :]
            lines = jnp.dot(pick, block, preferred_element_type=jnp.float32).astype(jnp.bfloat16)
            part = pl.ds(pl.multiple_of(i * 16, 16), 16)
            send_prs[0, part, :] = lines[:16, :]
            send_prs[1, part, :] = lines[16:, :]

        every(0, 2 * depth // 16, 1, step)
    load_prs.wait()
    pack_pressures()

    def shift_rows(first, count):
        part = jnp.concatenate([surf[g, first : first + count, :] for g in range(n_gz)], axis=1)
        wide_y = lax.broadcasted_iota(jnp.int32, part.shape, 1)
        for b in range(SIDE):
            off = b - HALF
            turned = part if off == 0 else pltpu.roll(part, (-off) % rows, 1)
            if off > 0:
                turned = jnp.where(wide_y < rows - off, turned, 0.0)
            if off < 0:
                turned = jnp.where(wide_y >= -off, turned, 0.0)
            put(shifted, pl.ds(first * SIDE + b, count, stride=SIDE), turned)

    shift_rows(HALF, cols)
    for s in range(2):

        @pl.when(has[s])
        def _():
            edge_arrival(s).wait_recv()
            prs_leave(s).start()

    for s in range(2):
        shift_rows(s * (HALF + cols), HALF)
    for h in range(2):
        for q in range(4):
            piece = get(shifted, pl.ds(h * 8 * SIDE + q * 128, 128))
            hi = piece.astype(jnp.bfloat16)
            rhs_hi[h, pl.ds(q * 128, 128), :] = hi
            rhs_lo[h, pl.ds(q * 128, 128), :] = (piece - hi.astype(jnp.float32)).astype(
                jnp.bfloat16
            )

    def product(i):
        tile = pl.ds(pl.multiple_of(i * 256, 256), 256)
        for h in range(2):
            src[h, tile, :] = (
                jnp.dot(toep_hi[tile, :], rhs_hi[h], preferred_element_type=jnp.float32)
                + jnp.dot(toep_hi[tile, :], rhs_lo[h], preferred_element_type=jnp.float32)
                + jnp.dot(toep_lo[tile, :], rhs_hi[h], preferred_element_type=jnp.float32)
            )

    every(0, depth * 8 // 256, 1, product)

    def chain(state, i, below):
        z = depth - 1 - i
        eight = pl.ds(pl.multiple_of(z * 8, 8), 8)
        solved = []
        for h in range(2):
            at = pl.multiple_of(z * cols + 8 * h, 8)
            part = pl.ds(at, 8)
            across = get(fx, pl.ds(pl.multiple_of(at + 8, 8), 8)) - get(fx, pl.ds(at + 7, 8))
            e = (get(state, part) + flux_y[part, :]) + (across + src[h, eight, :])
            e = e + edge_rows(edge_flux, z, h, rows)
            v = below[h] + rec[part, :] * (e - below[h])
            put(low, part, v)
            solved.append(v)
        return tuple(solved)

    for s in range(2):

        @pl.when(has[s])
        def _():
            top_come(s).wait_recv()
            halo_come(s).wait_recv()

    edges(0)
    nothing = (jnp.zeros((8, rows), jnp.float32),) * 2
    lax.fori_loop(0, depth, functools.partial(chain, adj), nothing, unroll=4)

    def inc_copy(level, to):
        return pltpu.make_async_remote_copy(
            src_ref=send_inc.at[level],
            dst_ref=recv_inc.at[level],
            send_sem=inc_send.at[level],
            recv_sem=inc_recv.at[level],
            device_id=(gx, to),
            device_id_type=MESH,
        )

    def relay(level):
        @pl.when(gz < n_gz - 1)
        def _():
            inc_copy(level, gz + 1).wait_recv()

        @pl.when(gz > 0)
        def _():
            first = pl.ds(0, cols)
            send_inc[level] = get(low, first) + get(dec, first) * recv_inc[level]
            inc_copy(level, gz - 1).start()

    early = gz < n_gz // 2

    @pl.when(early)
    def _():
        face_terms(0, False, False)
        every(0, depth, UNROLL, prepare_terms)

    relay(0)

    def pack_mid(i):
        z0 = pl.multiple_of(i * 16, 16)
        r0 = pl.multiple_of(i * 16 * cols, 16 * cols)
        for s in range(2):
            x = s * (cols - 1)
            line = pl.ds(r0 + x, 16, stride=cols)
            value = get(low, line) + get(dec, line) * recv_inc[0, x : x + 1, :]
            near_adj[1, s, pl.ds(z0, 16), :] = value
            send_mid[s, pl.ds(z0, 16), :] = value.astype(jnp.bfloat16)

    every(0, depth // 16, 2, pack_mid)

    for s in range(2):

        @pl.when(has[s])
        def _():
            mid_leave(s).start()

    below_next = pltpu.roll(recv_inc[0], cols - 1, 0)

    def level_second(z):
        at = pl.multiple_of(z * cols, cols)
        here = pl.ds(at, cols)
        a = get(low, here) + get(dec, here) * recv_inc[0]
        a_next = next_x(low, at) + next_x(dec, at) * below_next
        put(mid, here, a)
        lateral(1, a, a_next, at, tx[here, :], ty[here, :])

    every(0, depth, UNROLL, level_second)
    every(0, cells // block, 4, flux_steps)

    @pl.when(early)
    def _():
        face_terms(1, True, True)

    @pl.when(jnp.logical_not(early))
    def _():
        face_terms(1, False, False)

    for s in range(2):

        @pl.when(has[s])
        def _():
            mid_come(s).wait_recv()

    edges(1)
    lax.fori_loop(0, depth, functools.partial(chain, mid), nothing, unroll=4)
    relay(1)

    @pl.when(jnp.logical_not(early))
    def _():
        face_terms(0, True, False)

    for s in range(2):

        @pl.when(has[s])
        def _():
            prs_come(s).wait_recv()

    edge_terms()

    inc_ref[...] = recv_inc[1]

    for j in range(1, n_gz):
        surf_copy(j).wait_send()
    for s in range(2):

        @pl.when(has[s])
        def _():
            top_leave(s).wait_send()
            halo_leave(s).wait_send()
            prs_leave(s).wait_send()
            edge_copy(s).wait_send()
            mid_leave(s).wait_send()

    @pl.when(gz > 0)
    def _():
        inc_copy(0, gz - 1).wait_send()
        inc_copy(1, gz - 1).wait_send()


def on_device(
    n_gx,
    n_gz,
    residual,
    whitening,
    kernel,
    adjoint_end,
    pressure,
    log_permeability,
    vertical,
    top_layer,
    well_columns,
):
    depth, cols, rows = adjoint_end.shape
    cells = depth * cols
    f32, b16 = jnp.float32, jnp.bfloat16
    lanes = rows // LANES
    vmem = pltpu.VMEM
    field = vmem((cells, rows), f32)
    banded = vmem((lanes, cells + 8, LANES), f32)
    dma = pltpu.SemaphoreType.DMA
    wide = cols + 2 * HALF
    hbm = pl.BlockSpec(memory_space=pl.ANY)
    in_vmem = pl.BlockSpec(memory_space=vmem)
    kept = (
        banded,
        banded,
        vmem((cols, rows), f32),
        banded,
        field,
        banded,
        vmem((2, lanes, depth, LANES), f32),
        vmem((cols, rows), f32),
    )
    state = pl.pallas_call(
        functools.partial(window_kernel, n_gx, n_gz, depth, cols, rows),
        out_shape=kept,
        in_specs=[hbm] * 9,
        out_specs=(in_vmem,) * len(kept),
        scratch_shapes=[
            vmem(residual.shape, f32),
            vmem(whitening.shape, f32),
            vmem(kernel.shape, f32),
            vmem(top_layer.shape, jnp.int32),
            pltpu.SMEM(well_columns.shape, jnp.int32),
            banded,
            vmem((2 * cells, rows), b16),
            banded,
            vmem((cells, rows), b16),
            field,
            field,
            field,
            banded,
            vmem((cells, rows), b16),
            field,
            vmem((2, cells, rows), f32),
            banded,
            field,
            field,
            field,
            field,
            banded,
            vmem((2, depth * 8, rows), f32),
            vmem((n_gz, wide, rows // n_gz), f32),
            vmem((lanes, 8 * SIDE + 512, LANES), f32),
            vmem((2, 512, rows), b16),
            vmem((2, 512, rows), b16),
            vmem((depth, 512), f32),
            vmem((4, depth * 8, LANES), f32),
            vmem((depth * 8, 512), b16),
            vmem((depth * 8, 512), b16),
            vmem((3, cols, rows), f32),
            vmem((2, 2, depth, rows), f32),
            vmem((2, depth, rows), f32),
            vmem((2, lanes, depth, LANES), f32),
            vmem((rows, rows // 2), b16),
            vmem((rows, rows // 2), b16),
            vmem((2, 2 * depth, rows), b16),
            vmem((2, 2 * depth, rows), b16),
            vmem((2, 2 * depth, rows), b16),
            vmem((2, 2 * depth, rows), b16),
            vmem((2, 8, rows), f32),
            vmem((2, 8, rows), f32),
            vmem((2, depth, rows), b16),
            vmem((2, depth, rows), b16),
            vmem((2, cols, rows), f32),
            vmem((2, cols, rows), f32),
            dma((6,)),
            dma((CHUNKS, 1 + 2 * lanes)),
            dma((n_gz - 1,)),
            dma((n_gz - 1,)),
        ]
        + [dma((2,))] * 12,
        compiler_params=pltpu.CompilerParams(
            collective_id=0, has_side_effects=True, vmem_limit_bytes=50 * 1024 * 1024
        ),
    )(
        residual,
        whitening,
        kernel,
        top_layer,
        well_columns,
        adjoint_end.reshape(cells, rows),
        pressure.reshape(2 * cells, rows),
        log_permeability.reshape(cells, rows),
        vertical.reshape(cells, rows),
    )
    adjoint_start, gradient = pl.pallas_call(
        functools.partial(finish_kernel, n_gx, depth, cols, rows),
        out_shape=(jax.ShapeDtypeStruct((cells, rows), f32),) * 2,
        in_specs=[in_vmem] * len(kept),
        out_specs=(hbm, hbm),
        scratch_shapes=[field, field, dma((STORES, 2))],
        compiler_params=pltpu.CompilerParams(vmem_limit_bytes=8 * 1024 * 1024),
    )(*state)
    shape = (depth, cols, rows)
    return adjoint_start.reshape(shape), gradient.reshape(shape)


def solution(mesh):
    in_specs = (
        P("gx", "gz"),
        P("gx", "gz"),
        P("gz", None),
        P("gz", "gx", None),
        P(None, "gz", "gx", None),
        P("gz", "gx", None),
        P("gz", "gx", None),
        P("gx", None),
        P(),
    )
    out_specs = (P("gz", "gx", None), P("gz", "gx", None))
    return jax.shard_map(
        functools.partial(on_device, mesh.shape["gx"], mesh.shape["gz"]),
        mesh=mesh,
        in_specs=in_specs,
        out_specs=out_specs,
        check_vma=False,
    )
```

```python
import functools

import jax
import jax.numpy as jnp
from jax import lax
from jax.experimental import pallas as pl
from jax.experimental.pallas import tpu as pltpu
from jax.sharding import PartitionSpec as P

STEP_SIZE = 0.1
HALF = 8
SIDE = 17
FAR = 1e6
MESH = pl.DeviceIdType.MESH
CHUNKS = 1
UNROLL = 4
STORES = 8
SPLIT = 48
LANES = 128


def get(ref, at):
    return jnp.concatenate([ref[q, at, :] for q in range(ref.shape[0])], axis=1)


def put(ref, at, value):
    for q in range(ref.shape[0]):
        ref[q, at, :] = value[:, q * LANES : (q + 1) * LANES]


def every(low, high, unroll, body):
    def step(i, carry):
        body(i)
        return carry

    lax.fori_loop(low, high, step, 0, unroll=unroll)


def edge_rows(ref, z, h, rows):
    row_id = lax.broadcasted_iota(jnp.int32, (8, rows), 0)
    return jnp.where(row_id == 7 * h, get(ref.at[h], pl.ds(z, 1)), 0.0)


def finish_kernel(
    n_gx,
    depth,
    cols,
    rows,
    low,
    dec,
    inc_ref,
    gx_sum,
    gy_sum,
    mob,
    edge_term,
    top_ref,
    out_hbm,
    grad_hbm,
    out,
    grad,
    sem,
):
    z_base = lax.axis_index("gz") * depth
    chunk = depth // STORES

    def finish(z):
        at = pl.multiple_of(z * cols, cols)
        here = pl.ds(at, cols)
        live = top_ref[...] <= (z_base + z).astype(jnp.float32)
        out[here, :] = jnp.where(live, get(low, here) + get(dec, here) * inc_ref[...], 0.0)
        across = get(gx_sum, pl.ds(pl.multiple_of(at + 8, 8), cols)) + get(
            gx_sum, pl.ds(at + 7, cols)
        )
        ends = jnp.concatenate([edge_rows(edge_term, z, h, rows) for h in range(2)], axis=0)
        grad[here, :] = get(mob, here) * ((gy_sum[here, :] + across) + ends)

    def stores(c):
        part = pl.ds(c * chunk * cols, chunk * cols)
        return [
            pltpu.make_async_copy(a.at[part], b.at[part], sem.at[c, i])
            for i, (a, b) in enumerate(((out, out_hbm), (grad, grad_hbm)))
        ]

    pending = []
    for c in range(STORES):
        every(c * chunk, (c + 1) * chunk, 4, finish)
        copies = stores(c)
        for copy in copies:
            copy.start()
        pending += copies
    for copy in pending:
        copy.wait()


def window_kernel(
    n_gx,
    n_gz,
    depth,
    cols,
    rows,
    residual_hbm,
    whitening_hbm,
    kernel_hbm,
    top_hbm,
    wells_hbm,
    adjoint_hbm,
    pressure_hbm,
    logk_hbm,
    vertical_hbm,
    low,
    dec,
    inc_ref,
    gx_sum,
    gy_sum,
    mob,
    edge_term,
    top_out,
    residual_ref,
    whitening_ref,
    kernel_ref,
    top_ref,
    wells_ref,
    adj,
    prs,
    logk,
    ver,
    tx,
    ty,
    face_y,
    fx,
    fy_narrow,
    flux_y,
    steps_y,
    gx_part,
    gy_part,
    step_x,
    step_y,
    rec,
    mid,
    src,
    surf,
    shifted,
    rhs_hi,
    rhs_lo,
    kpad,
    toep,
    toep_hi,
    toep_lo,
    tops,
    near_adj,
    near_mob,
    edge_flux,
    pair_sum,
    pair_step,
    send_halo,
    recv_halo,
    send_prs,
    recv_prs,
    send_top,
    recv_top,
    send_mid,
    recv_mid,
    send_inc,
    recv_inc,
    small_sem,
    load_sem,
    surf_send,
    surf_recv,
    edge_send,
    edge_recv,
    halo_send,
    halo_recv,
    prs_send,
    prs_recv,
    top_send,
    top_recv,
    mid_send,
    mid_recv,
    inc_send,
    inc_recv,
):
    gx = lax.axis_index("gx")
    gz = lax.axis_index("gz")
    layers = depth // CHUNKS
    span = layers * cols
    cells = depth * cols
    bands = rows // LANES
    has = (gx > 0, gx < n_gx - 1)
    beside = (gx - 1, gx + 1)

    barrier = pltpu.get_barrier_semaphore()
    for j in range(1, n_gz):
        pl.semaphore_signal(
            barrier, inc=1, device_id=(gx, lax.rem(gz + j, n_gz)), device_id_type=MESH
        )
    for s in range(2):

        @pl.when(has[s])
        def _():
            pl.semaphore_signal(barrier, inc=1, device_id=(beside[s], gz), device_id_type=MESH)

    small = [
        pltpu.make_async_copy(a, b, small_sem.at[i])
        for i, (a, b) in enumerate(
            (
                (residual_hbm, residual_ref),
                (whitening_hbm, whitening_ref),
                (top_hbm, top_ref),
                (wells_hbm, wells_ref),
                (kernel_hbm, kernel_ref),
            )
        )
    ]
    for copy in small:
        copy.start()

    def loads(c):
        at = c * span
        here = pl.ds(at, span)
        pairs = []
        for q in range(bands):
            lane = pl.ds(q * LANES, LANES)
            pairs.append((logk_hbm.at[here, lane], logk.at[q, here]))
            pairs.append((adjoint_hbm.at[here, lane], adj.at[q, here]))
        pairs.append((vertical_hbm.at[here], ver.at[here]))
        return [
            pltpu.make_async_copy(a, b, load_sem.at[c, i]) for i, (a, b) in enumerate(pairs)
        ]

    chunk_loads = [loads(c) for c in range(CHUNKS)]
    for copies in reversed(chunk_loads):
        for copy in copies[: 2 * bands]:
            copy.start()
    for copies in reversed(chunk_loads):
        copies[2 * bands].start()
    load_prs = pltpu.make_async_copy(pressure_hbm, prs, small_sem.at[5])
    load_prs.start()

    for s in range(2):

        @pl.when(jnp.logical_not(has[s]))
        def _():
            first = s * (HALF + cols)
            surf[:, first : first + HALF, :] = jnp.zeros((n_gz, HALF, rows // n_gz), jnp.float32)
            recv_halo[s] = jnp.zeros(recv_halo.shape[1:], recv_halo.dtype)
            recv_top[s] = jnp.full(recv_top.shape[1:], FAR, jnp.float32)
            recv_mid[s] = jnp.zeros(recv_mid.shape[1:], recv_mid.dtype)
            recv_prs[s] = jnp.zeros(recv_prs.shape[1:], recv_prs.dtype)

    @pl.when(gz == n_gz - 1)
    def _():
        recv_inc[...] = jnp.zeros(recv_inc.shape, jnp.float32)

    blank = jnp.zeros((8, rows), jnp.float32)
    after = pl.ds(cells, 8)
    for ref in (mob, adj, low, dec, mid, logk):
        put(ref, after, blank)
    for ref in (fx, gx_sum, gx_part):
        put(ref, pl.ds(0, 8), blank)

    small[0].wait()
    small[1].wait()
    strip = surf.at[gz]
    strip[HALF : HALF + cols, :] = residual_ref[...] * whitening_ref[...]

    small[2].wait()
    small[3].wait()
    cell = (
        (gx * cols + lax.broadcasted_iota(jnp.int32, (cols, rows), 0)) * rows
        + lax.broadcasted_iota(jnp.int32, (cols, rows), 1)
    )

    def drill(i, top):
        return jnp.where(cell == wells_ref[i], FAR, top)

    top = lax.fori_loop(
        0, wells_ref.shape[0], drill, top_ref[...].astype(jnp.float32), unroll=8
    )
    x_id = lax.broadcasted_iota(jnp.int32, (cols, rows), 0)
    y_id = lax.broadcasted_iota(jnp.int32, (cols, rows), 1)
    tops[0] = top
    top_out[...] = top
    tops[1] = jnp.where(x_id == cols - 1, FAR, jnp.maximum(top, pltpu.roll(top, cols - 1, 0)))
    tops[2] = jnp.where(y_id == rows - 1, FAR, jnp.maximum(top, pltpu.roll(top, rows - 1, 1)))
    send_top[0] = jnp.broadcast_to(top[0:1, :], (8, rows))
    send_top[1] = jnp.broadcast_to(top[cols - 1 : cols, :], (8, rows))

    small[4].wait()
    kpad[...] = jnp.zeros(kpad.shape, jnp.float32)
    kpad[:, 0 : SIDE * SIDE] = kernel_ref[...]
    for x in range(8):
        put(toep, pl.ds(x, depth, stride=8), pltpu.roll(kpad[...], SIDE * x, 1))
    tail = shifted.shape[1] - (cols + 2 * HALF) * SIDE
    put(shifted, pl.ds((cols + 2 * HALF) * SIDE, tail), jnp.zeros((tail, rows), jnp.float32))

    def halve(i):
        tile = pl.ds(pl.multiple_of(i * 64, 64), 64)
        piece = get(toep, tile)
        hi = piece.astype(jnp.bfloat16)
        toep_hi[tile, :] = hi
        toep_lo[tile, :] = (piece - hi.astype(jnp.float32)).astype(jnp.bfloat16)

    every(0, depth * 8 // 64, 4, halve)

    tile = rows // 2
    k_id = lax.broadcasted_iota(jnp.int32, (rows, tile), 0)
    n_id = lax.broadcasted_iota(jnp.int32, (rows, tile), 1)
    same, nearby = k_id == n_id, k_id == n_id + 1
    pair_sum[...] = jnp.where(same, 1.0, jnp.where(nearby, 1.0, 0.0)).astype(jnp.bfloat16)
    same, nearby = k_id == n_id + tile, k_id + 1 == n_id + tile
    pair_step[...] = jnp.where(same, 1.0, jnp.where(nearby, -1.0, 0.0)).astype(jnp.bfloat16)

    block = 16 * cols

    def product_of(lhs, rhs):
        return jnp.dot(lhs, rhs, preferred_element_type=jnp.float32)

    def mobilities(i):
        at = pl.ds(pl.multiple_of(i * block, block), block)
        m = (0.5 * STEP_SIZE) * jnp.exp(get(logk, at))
        put(mob, at, m)
        m = m.astype(jnp.bfloat16)
        face_y[at, :tile] = product_of(m, pair_sum[...])
        face_y[at, tile:] = product_of(m[:, tile:], pair_sum[:tile, :])

    def flux_steps(i):
        at = pl.ds(pl.multiple_of(i * block, block), block)
        f = fy_narrow[at, :]
        flux_y[at, :tile] = product_of(f[:, :tile], pair_step[tile:, :])
        flux_y[at, tile:] = product_of(f, pair_step[...])

    for c in reversed(range(CHUNKS)):
        for copy in chunk_loads[c][: 2 * bands]:
            copy.wait()
        every(c * span // block, (c + 1) * span // block, 4, mobilities)

    strips_beside = jnp.where(has[0], 1, 0) + jnp.where(has[1], 1, 0)
    pl.semaphore_wait(barrier, n_gz - 1 + strips_beside)

    def surf_copy(j):
        mine = surf.at[gz, pl.ds(HALF, cols), :]
        return pltpu.make_async_remote_copy(
            src_ref=mine,
            dst_ref=mine,
            send_sem=surf_send.at[j - 1],
            recv_sem=surf_recv.at[j - 1],
            device_id=(gx, lax.rem(gz + j, n_gz)),
            device_id_type=MESH,
        )

    def surf_arrival(j):
        theirs = surf.at[lax.rem(gz + n_gz - j, n_gz), pl.ds(HALF, cols), :]
        return pltpu.make_async_remote_copy(
            src_ref=theirs,
            dst_ref=theirs,
            send_sem=surf_send.at[j - 1],
            recv_sem=surf_recv.at[j - 1],
            device_id=(gx, lax.rem(gz + j, n_gz)),
            device_id_type=MESH,
        )

    for j in range(1, n_gz):
        surf_copy(j).start()

    def pack(i):
        z0 = pl.multiple_of(i * 16, 16)
        r0 = pl.multiple_of(i * 16 * cols, 16 * cols)
        for s in range(2):
            line = pl.ds(r0 + s * (cols - 1), 16, stride=cols)
            fields = (get(adj, line), get(mob, line))
            near_adj[0, s, pl.ds(z0, 16), :] = fields[0]
            near_mob[s, pl.ds(z0, 16), :] = fields[1]
            for k, field in enumerate(fields):
                send_halo[s, pl.ds(k * depth + z0, 16), :] = field.astype(jnp.bfloat16)

    every(0, depth // 16, 2, pack)

    def swap(sent, arrived, send_sem, recv_sem):
        def leave(s):
            return pltpu.make_async_remote_copy(
                src_ref=sent.at[s],
                dst_ref=arrived.at[1 - s],
                send_sem=send_sem.at[s],
                recv_sem=recv_sem.at[1 - s],
                device_id=(beside[s], gz),
                device_id_type=MESH,
            )

        def come(s):
            return pltpu.make_async_remote_copy(
                src_ref=sent.at[1 - s],
                dst_ref=arrived.at[s],
                send_sem=send_sem.at[1 - s],
                recv_sem=recv_sem.at[s],
                device_id=(beside[s], gz),
                device_id_type=MESH,
            )

        return leave, come

    top_leave, top_come = swap(send_top, recv_top, top_send, top_recv)
    halo_leave, halo_come = swap(send_halo, recv_halo, halo_send, halo_recv)
    prs_leave, prs_come = swap(send_prs, recv_prs, prs_send, prs_recv)
    mid_leave, mid_come = swap(send_mid, recv_mid, mid_send, mid_recv)

    for s in range(2):

        @pl.when(has[s])
        def _():
            top_leave(s).start()
            halo_leave(s).start()

    z_base = gz * depth

    def next_x(ref, at):
        return get(ref, pl.ds(at + 1, cols))

    def next_y(value):
        return pltpu.roll(value, rows - 1, 1)

    def lower(at):
        return pl.ds(pl.multiple_of(at + 8, 8), cols)

    def lateral(level, a, a_next, at, open_x, open_y):
        here = pl.ds(at, cols)
        put(fx, lower(at), open_x * (a_next - a))
        dy = next_y(a) - a
        steps_y[level, here, :] = dy
        fy_narrow[here, :] = (open_y * dy).astype(jnp.bfloat16)

    def level_first(i, decay):
        z = depth - 1 - i
        at = pl.multiple_of(z * cols, cols)
        here = pl.ds(at, cols)
        zf = (z_base + z).astype(jnp.float32)
        open_x = jnp.where(tops[1] <= zf, get(mob, here) + next_x(mob, at), 0.0)
        open_y = jnp.where(tops[2] <= zf, face_y[here, :], 0.0)
        tx[here, :] = open_x
        ty[here, :] = open_y
        lateral(0, get(adj, here), next_x(adj, at), at, open_x, open_y)
        r = jnp.where(tops[0] <= zf, 1.0 / (1.0 + ver[here, :].astype(jnp.float32)), 0.0)
        rec[here, :] = r
        decay = decay - r * decay
        put(dec, here, decay)
        return decay

    decay = jnp.ones((cols, rows), jnp.float32)
    for c in range(CHUNKS):
        chunk_loads[c][2 * bands].wait()
    decay = lax.fori_loop(0, SPLIT, level_first, decay, unroll=UNROLL)

    def edge_copy(s):
        first = HALF + s * (cols - HALF)
        return pltpu.make_async_remote_copy(
            src_ref=surf.at[:, pl.ds(first, HALF), :],
            dst_ref=surf.at[:, pl.ds((1 - s) * (HALF + cols), HALF), :],
            send_sem=edge_send.at[s],
            recv_sem=edge_recv.at[1 - s],
            device_id=(beside[s], gz),
            device_id_type=MESH,
        )

    def edge_arrival(s):
        first = HALF + (1 - s) * (cols - HALF)
        return pltpu.make_async_remote_copy(
            src_ref=surf.at[:, pl.ds(first, HALF), :],
            dst_ref=surf.at[:, pl.ds(s * (HALF + cols), HALF), :],
            send_sem=edge_send.at[1 - s],
            recv_sem=edge_recv.at[s],
            device_id=(beside[s], gz),
            device_id_type=MESH,
        )

    for j in range(1, n_gz):
        surf_arrival(j).wait_recv()
    for s in range(2):

        @pl.when(has[s])
        def _():
            edge_copy(s).start()

    lax.fori_loop(SPLIT, depth, level_first, decay, unroll=UNROLL)
    every(0, cells // block, 4, flux_steps)

    def side_steps(level, s, i):
        z0 = pl.multiple_of(i * 16, 16)
        part = pl.ds(z0, 16)
        x = s * (cols - 1)
        zf = (z_base + z0 + lax.broadcasted_iota(jnp.int32, (16, rows), 0)).astype(jnp.float32)
        far = (recv_halo if level == 0 else recv_mid)[s, part, :].astype(jnp.float32)
        face = jnp.maximum(tops[0, x : x + 1, :], recv_top[s, 0:1, :])
        return part, jnp.where(face <= zf, far - near_adj[level, s, part, :], 0.0)

    def edges(level):
        def step(i):
            for s in range(2):
                part, d = side_steps(level, s, i)
                far_m = recv_halo[s, pl.ds(pl.multiple_of(depth + i * 16, 16), 16), :]
                put(edge_flux.at[s], part, (near_mob[s, part, :] + far_m.astype(jnp.float32)) * d)

        every(0, depth // 16, 4, step)

    def edge_terms():
        def step(i):
            for s in range(2):
                total = None
                for level in range(2):
                    part, d = side_steps(level, s, i)
                    p_part = pl.ds(pl.multiple_of(level * depth + i * 16, 16), 16)
                    far_p = recv_prs[s, p_part, :].astype(jnp.float32)
                    term = d * (far_p - send_prs[s, p_part, :].astype(jnp.float32))
                    total = term if total is None else total + term
                put(edge_term.at[s], part, total)

        every(0, depth // 16, 4, step)

    def pressure_steps(level, z, at):
        zf = (z_base + z).astype(jnp.float32)
        p = prs[pl.ds(pl.multiple_of(level * cells + at, cols), cols), :].astype(jnp.float32)
        across = jnp.where(tops[1] <= zf, pltpu.roll(p, cols - 1, 0) - p, 0.0)
        return across, jnp.where(tops[2] <= zf, next_y(p) - p, 0.0)

    def prepare_terms(z):
        at = pl.multiple_of(z * cols, cols)
        across, along = pressure_steps(1, z, at)
        step_x[pl.ds(at, cols), :] = across
        step_y[pl.ds(at, cols), :] = along

    def face_terms(level, add, ready):
        state = (adj, mid)[level]

        def step(z):
            at = pl.multiple_of(z * cols, cols)
            here = pl.ds(at, cols)
            if ready:
                across, along = step_x[here, :], step_y[here, :]
            else:
                across, along = pressure_steps(level, z, at)
            term_x = (next_x(state, at) - get(state, here)) * across
            term_y = steps_y[level, here, :] * along
            if add:
                term_x = term_x + get(gx_part, lower(at))
                term_y = term_y + gy_part[here, :]
                gy_sum[here, :] = term_y + pltpu.roll(term_y, 1, 1)
            else:
                gy_part[here, :] = term_y
            put(gx_sum if add else gx_part, lower(at), term_x)

        every(0, depth, UNROLL, step)

    def pack_pressures():
        z_of = lax.broadcasted_iota(jnp.int32, (32, 256), 0)
        k_of = lax.broadcasted_iota(jnp.int32, (32, 256), 1)
        pick = (k_of == jnp.where(z_of < 16, z_of * cols, z_of * cols - 15 * cols - 1)).astype(
            jnp.bfloat16
        )

        def step(i):
            block = prs[pl.ds(pl.multiple_of(i * 256, 256), 256), :]
            lines = jnp.dot(pick, block, preferred_element_type=jnp.float32).astype(jnp.bfloat16)
            part = pl.ds(pl.multiple_of(i * 16, 16), 16)
            send_prs[0, part, :] = lines[:16, :]
            send_prs[1, part, :] = lines[16:, :]

        every(0, 2 * depth // 16, 1, step)
    load_prs.wait()
    pack_pressures()

    def shift_rows(first, count):
        part = jnp.concatenate([surf[g, first : first + count, :] for g in range(n_gz)], axis=1)
        wide_y = lax.broadcasted_iota(jnp.int32, part.shape, 1)
        for b in range(SIDE):
            off = b - HALF
            turned = part if off == 0 else pltpu.roll(part, (-off) % rows, 1)
            if off > 0:
                turned = jnp.where(wide_y < rows - off, turned, 0.0)
            if off < 0:
                turned = jnp.where(wide_y >= -off, turned, 0.0)
            put(shifted, pl.ds(first * SIDE + b, count, stride=SIDE), turned)

    shift_rows(HALF, cols)
    for s in range(2):

        @pl.when(has[s])
        def _():
            edge_arrival(s).wait_recv()
            prs_leave(s).start()

    for s in range(2):
        shift_rows(s * (HALF + cols), HALF)
    for h in range(2):
        for q in range(4):
            piece = get(shifted, pl.ds(h * 8 * SIDE + q * 128, 128))
            hi = piece.astype(jnp.bfloat16)
            rhs_hi[h, pl.ds(q * 128, 128), :] = hi
            rhs_lo[h, pl.ds(q * 128, 128), :] = (piece - hi.astype(jnp.float32)).astype(
                jnp.bfloat16
            )

    def product(i):
        tile = pl.ds(pl.multiple_of(i * 256, 256), 256)
        for h in range(2):
            src[h, tile, :] = (
                jnp.dot(toep_hi[tile, :], rhs_hi[h], preferred_element_type=jnp.float32)
                + jnp.dot(toep_hi[tile, :], rhs_lo[h], preferred_element_type=jnp.float32)
                + jnp.dot(toep_lo[tile, :], rhs_hi[h], preferred_element_type=jnp.float32)
            )

    every(0, depth * 8 // 256, 2, product)

    def chain(state, i, below):
        z = depth - 1 - i
        eight = pl.ds(pl.multiple_of(z * 8, 8), 8)
        solved = []
        for h in range(2):
            at = pl.multiple_of(z * cols + 8 * h, 8)
            part = pl.ds(at, 8)
            across = get(fx, pl.ds(pl.multiple_of(at + 8, 8), 8)) - get(fx, pl.ds(at + 7, 8))
            e = (get(state, part) + flux_y[part, :]) + (across + src[h, eight, :])
            e = e + edge_rows(edge_flux, z, h, rows)
            v = below[h] + rec[part, :] * (e - below[h])
            put(low, part, v)
            solved.append(v)
        return tuple(solved)

    for s in range(2):

        @pl.when(has[s])
        def _():
            top_come(s).wait_recv()
            halo_come(s).wait_recv()

    edges(0)
    nothing = (jnp.zeros((8, rows), jnp.float32),) * 2
    lax.fori_loop(0, depth, functools.partial(chain, adj), nothing, unroll=4)

    def inc_copy(level, to):
        return pltpu.make_async_remote_copy(
            src_ref=send_inc.at[level],
            dst_ref=recv_inc.at[level],
            send_sem=inc_send.at[level],
            recv_sem=inc_recv.at[level],
            device_id=(gx, to),
            device_id_type=MESH,
        )

    def relay(level):
        @pl.when(gz < n_gz - 1)
        def _():
            inc_copy(level, gz + 1).wait_recv()

        @pl.when(gz > 0)
        def _():
            first = pl.ds(0, cols)
            send_inc[level] = get(low, first) + get(dec, first) * recv_inc[level]
            inc_copy(level, gz - 1).start()

    early = gz < n_gz // 2

    @pl.when(early)
    def _():
        face_terms(0, False, False)
        every(0, depth, UNROLL, prepare_terms)

    relay(0)

    def pack_mid(i):
        z0 = pl.multiple_of(i * 16, 16)
        r0 = pl.multiple_of(i * 16 * cols, 16 * cols)
        for s in range(2):
            x = s * (cols - 1)
            line = pl.ds(r0 + x, 16, stride=cols)
            value = get(low, line) + get(dec, line) * recv_inc[0, x : x + 1, :]
            near_adj[1, s, pl.ds(z0, 16), :] = value
            send_mid[s, pl.ds(z0, 16), :] = value.astype(jnp.bfloat16)

    every(0, depth // 16, 4, pack_mid)

    for s in range(2):

        @pl.when(has[s])
        def _():
            mid_leave(s).start()

    below_next = pltpu.roll(recv_inc[0], cols - 1, 0)

    def level_second(z):
        at = pl.multiple_of(z * cols, cols)
        here = pl.ds(at, cols)
        a = get(low, here) + get(dec, here) * recv_inc[0]
        a_next = next_x(low, at) + next_x(dec, at) * below_next
        put(mid, here, a)
        lateral(1, a, a_next, at, tx[here, :], ty[here, :])

    every(0, depth, UNROLL, level_second)
    every(0, cells // block, 4, flux_steps)

    @pl.when(early)
    def _():
        face_terms(1, True, True)

    @pl.when(jnp.logical_not(early))
    def _():
        face_terms(1, False, False)

    for s in range(2):

        @pl.when(has[s])
        def _():
            mid_come(s).wait_recv()

    edges(1)
    lax.fori_loop(0, depth, functools.partial(chain, mid), nothing, unroll=4)
    relay(1)

    @pl.when(jnp.logical_not(early))
    def _():
        face_terms(0, True, False)

    for s in range(2):

        @pl.when(has[s])
        def _():
            prs_come(s).wait_recv()

    edge_terms()

    inc_ref[...] = recv_inc[1]

    for j in range(1, n_gz):
        surf_copy(j).wait_send()
    for s in range(2):

        @pl.when(has[s])
        def _():
            top_leave(s).wait_send()
            halo_leave(s).wait_send()
            prs_leave(s).wait_send()
            edge_copy(s).wait_send()
            mid_leave(s).wait_send()

    @pl.when(gz > 0)
    def _():
        inc_copy(0, gz - 1).wait_send()
        inc_copy(1, gz - 1).wait_send()


def on_device(
    n_gx,
    n_gz,
    residual,
    whitening,
    kernel,
    adjoint_end,
    pressure,
    log_permeability,
    vertical,
    top_layer,
    well_columns,
):
    depth, cols, rows = adjoint_end.shape
    cells = depth * cols
    f32, b16 = jnp.float32, jnp.bfloat16
    lanes = rows // LANES
    vmem = pltpu.VMEM
    field = vmem((cells, rows), f32)
    banded = vmem((lanes, cells + 8, LANES), f32)
    dma = pltpu.SemaphoreType.DMA
    wide = cols + 2 * HALF
    hbm = pl.BlockSpec(memory_space=pl.ANY)
    in_vmem = pl.BlockSpec(memory_space=vmem)
    kept = (
        banded,
        banded,
        vmem((cols, rows), f32),
        banded,
        field,
        banded,
        vmem((2, lanes, depth, LANES), f32),
        vmem((cols, rows), f32),
    )
    state = pl.pallas_call(
        functools.partial(window_kernel, n_gx, n_gz, depth, cols, rows),
        out_shape=kept,
        in_specs=[hbm] * 9,
        out_specs=(in_vmem,) * len(kept),
        scratch_shapes=[
            vmem(residual.shape, f32),
            vmem(whitening.shape, f32),
            vmem(kernel.shape, f32),
            vmem(top_layer.shape, jnp.int32),
            pltpu.SMEM(well_columns.shape, jnp.int32),
            banded,
            vmem((2 * cells, rows), b16),
            banded,
            vmem((cells, rows), b16),
            field,
            field,
            field,
            banded,
            vmem((cells, rows), b16),
            field,
            vmem((2, cells, rows), f32),
            banded,
            field,
            field,
            field,
            field,
            banded,
            vmem((2, depth * 8, rows), f32),
            vmem((n_gz, wide, rows // n_gz), f32),
            vmem((lanes, 8 * SIDE + 512, LANES), f32),
            vmem((2, 512, rows), b16),
            vmem((2, 512, rows), b16),
            vmem((depth, 512), f32),
            vmem((4, depth * 8, LANES), f32),
            vmem((depth * 8, 512), b16),
            vmem((depth * 8, 512), b16),
            vmem((3, cols, rows), f32),
            vmem((2, 2, depth, rows), f32),
            vmem((2, depth, rows), f32),
            vmem((2, lanes, depth, LANES), f32),
            vmem((rows, rows // 2), b16),
            vmem((rows, rows // 2), b16),
            vmem((2, 2 * depth, rows), b16),
            vmem((2, 2 * depth, rows), b16),
            vmem((2, 2 * depth, rows), b16),
            vmem((2, 2 * depth, rows), b16),
            vmem((2, 8, rows), f32),
            vmem((2, 8, rows), f32),
            vmem((2, depth, rows), b16),
            vmem((2, depth, rows), b16),
            vmem((2, cols, rows), f32),
            vmem((2, cols, rows), f32),
            dma((6,)),
            dma((CHUNKS, 1 + 2 * lanes)),
            dma((n_gz - 1,)),
            dma((n_gz - 1,)),
        ]
        + [dma((2,))] * 12,
        compiler_params=pltpu.CompilerParams(
            collective_id=0, has_side_effects=True, vmem_limit_bytes=50 * 1024 * 1024
        ),
    )(
        residual,
        whitening,
        kernel,
        top_layer,
        well_columns,
        adjoint_end.reshape(cells, rows),
        pressure.reshape(2 * cells, rows),
        log_permeability.reshape(cells, rows),
        vertical.reshape(cells, rows),
    )
    adjoint_start, gradient = pl.pallas_call(
        functools.partial(finish_kernel, n_gx, depth, cols, rows),
        out_shape=(jax.ShapeDtypeStruct((cells, rows), f32),) * 2,
        in_specs=[in_vmem] * len(kept),
        out_specs=(hbm, hbm),
        scratch_shapes=[field, field, dma((STORES, 2))],
        compiler_params=pltpu.CompilerParams(vmem_limit_bytes=8 * 1024 * 1024),
    )(*state)
    shape = (depth, cols, rows)
    return adjoint_start.reshape(shape), gradient.reshape(shape)


def solution(mesh):
    in_specs = (
        P("gx", "gz"),
        P("gx", "gz"),
        P("gz", None),
        P("gz", "gx", None),
        P(None, "gz", "gx", None),
        P("gz", "gx", None),
        P("gz", "gx", None),
        P("gx", None),
        P(),
    )
    out_specs = (P("gz", "gx", None), P("gz", "gx", None))
    return jax.shard_map(
        functools.partial(on_device, mesh.shape["gx"], mesh.shape["gz"]),
        mesh=mesh,
        in_specs=in_specs,
        out_specs=out_specs,
        check_vma=False,
    )
```

```python
import functools

import jax
import jax.numpy as jnp
from jax import lax
from jax.experimental import pallas as pl
from jax.experimental.pallas import tpu as pltpu
from jax.sharding import PartitionSpec as P

STEP_SIZE = 0.1
HALF = 8
SIDE = 17
FAR = 1e6
MESH = pl.DeviceIdType.MESH
CHUNKS = 1
UNROLL = 4
STORES = 8
SPLIT = 48
LANES = 128


def get(ref, at):
    return jnp.concatenate([ref[q, at, :] for q in range(ref.shape[0])], axis=1)


def put(ref, at, value):
    for q in range(ref.shape[0]):
        ref[q, at, :] = value[:, q * LANES : (q + 1) * LANES]


def every(low, high, unroll, body):
    def step(i, carry):
        body(i)
        return carry

    lax.fori_loop(low, high, step, 0, unroll=unroll)


def edge_rows(ref, z, h, rows):
    row_id = lax.broadcasted_iota(jnp.int32, (8, rows), 0)
    return jnp.where(row_id == 7 * h, get(ref.at[h], pl.ds(z, 1)), 0.0)


def finish_kernel(
    n_gx,
    depth,
    cols,
    rows,
    low,
    dec,
    inc_ref,
    gx_sum,
    gy_sum,
    mob,
    edge_term,
    top_ref,
    out_hbm,
    grad_hbm,
    out,
    grad,
    sem,
):
    z_base = lax.axis_index("gz") * depth
    chunk = depth // STORES

    def finish(z):
        at = pl.multiple_of(z * cols, cols)
        here = pl.ds(at, cols)
        live = top_ref[...] <= (z_base + z).astype(jnp.float32)
        out[here, :] = jnp.where(live, get(low, here) + get(dec, here) * inc_ref[...], 0.0)
        across = get(gx_sum, pl.ds(pl.multiple_of(at + 8, 8), cols)) + get(
            gx_sum, pl.ds(at + 7, cols)
        )
        ends = jnp.concatenate([edge_rows(edge_term, z, h, rows) for h in range(2)], axis=0)
        grad[here, :] = get(mob, here) * ((gy_sum[here, :] + across) + ends)

    def stores(c):
        part = pl.ds(c * chunk * cols, chunk * cols)
        return [
            pltpu.make_async_copy(a.at[part], b.at[part], sem.at[c, i])
            for i, (a, b) in enumerate(((out, out_hbm), (grad, grad_hbm)))
        ]

    pending = []
    for c in range(STORES):
        every(c * chunk, (c + 1) * chunk, 8, finish)
        copies = stores(c)
        for copy in copies:
            copy.start()
        pending += copies
    for copy in pending:
        copy.wait()


def window_kernel(
    n_gx,
    n_gz,
    depth,
    cols,
    rows,
    residual_hbm,
    whitening_hbm,
    kernel_hbm,
    top_hbm,
    wells_hbm,
    adjoint_hbm,
    pressure_hbm,
    logk_hbm,
    vertical_hbm,
    low,
    dec,
    inc_ref,
    gx_sum,
    gy_sum,
    mob,
    edge_term,
    top_out,
    residual_ref,
    whitening_ref,
    kernel_ref,
    top_ref,
    wells_ref,
    adj,
    prs,
    logk,
    ver,
    tx,
    ty,
    face_y,
    fx,
    fy_narrow,
    flux_y,
    steps_y,
    gx_part,
    gy_part,
    step_x,
    step_y,
    rec,
    mid,
    src,
    surf,
    shifted,
    rhs_hi,
    rhs_lo,
    kpad,
    toep,
    toep_hi,
    toep_lo,
    tops,
    near_adj,
    near_mob,
    edge_flux,
    pair_sum,
    pair_step,
    send_halo,
    recv_halo,
    send_prs,
    recv_prs,
    send_top,
    recv_top,
    send_mid,
    recv_mid,
    send_inc,
    recv_inc,
    small_sem,
    load_sem,
    surf_send,
    surf_recv,
    edge_send,
    edge_recv,
    halo_send,
    halo_recv,
    prs_send,
    prs_recv,
    top_send,
    top_recv,
    mid_send,
    mid_recv,
    inc_send,
    inc_recv,
):
    gx = lax.axis_index("gx")
    gz = lax.axis_index("gz")
    layers = depth // CHUNKS
    span = layers * cols
    cells = depth * cols
    bands = rows // LANES
    has = (gx > 0, gx < n_gx - 1)
    beside = (gx - 1, gx + 1)

    barrier = pltpu.get_barrier_semaphore()
    for j in range(1, n_gz):
        pl.semaphore_signal(
            barrier, inc=1, device_id=(gx, lax.rem(gz + j, n_gz)), device_id_type=MESH
        )
    for s in range(2):

        @pl.when(has[s])
        def _():
            pl.semaphore_signal(barrier, inc=1, device_id=(beside[s], gz), device_id_type=MESH)

    small = [
        pltpu.make_async_copy(a, b, small_sem.at[i])
        for i, (a, b) in enumerate(
            (
                (residual_hbm, residual_ref),
                (whitening_hbm, whitening_ref),
                (top_hbm, top_ref),
                (wells_hbm, wells_ref),
                (kernel_hbm, kernel_ref),
            )
        )
    ]
    for copy in small:
        copy.start()

    def loads(c):
        at = c * span
        here = pl.ds(at, span)
        pairs = []
        for q in range(bands):
            lane = pl.ds(q * LANES, LANES)
            pairs.append((logk_hbm.at[here, lane], logk.at[q, here]))
            pairs.append((adjoint_hbm.at[here, lane], adj.at[q, here]))
        pairs.append((vertical_hbm.at[here], ver.at[here]))
        return [
            pltpu.make_async_copy(a, b, load_sem.at[c, i]) for i, (a, b) in enumerate(pairs)
        ]

    chunk_loads = [loads(c) for c in range(CHUNKS)]
    for copies in reversed(chunk_loads):
        for copy in copies[: 2 * bands]:
            copy.start()
    for copies in reversed(chunk_loads):
        copies[2 * bands].start()
    load_prs = pltpu.make_async_copy(pressure_hbm, prs, small_sem.at[5])
    load_prs.start()

    for s in range(2):

        @pl.when(jnp.logical_not(has[s]))
        def _():
            first = s * (HALF + cols)
            surf[:, first : first + HALF, :] = jnp.zeros((n_gz, HALF, rows // n_gz), jnp.float32)
            recv_halo[s] = jnp.zeros(recv_halo.shape[1:], recv_halo.dtype)
            recv_top[s] = jnp.full(recv_top.shape[1:], FAR, jnp.float32)
            recv_mid[s] = jnp.zeros(recv_mid.shape[1:], recv_mid.dtype)
            recv_prs[s] = jnp.zeros(recv_prs.shape[1:], recv_prs.dtype)

    @pl.when(gz == n_gz - 1)
    def _():
        recv_inc[...] = jnp.zeros(recv_inc.shape, jnp.float32)

    blank = jnp.zeros((8, rows), jnp.float32)
    after = pl.ds(cells, 8)
    for ref in (mob, adj, low, dec, mid, logk):
        put(ref, after, blank)
    for ref in (fx, gx_sum, gx_part):
        put(ref, pl.ds(0, 8), blank)

    small[0].wait()
    small[1].wait()
    strip = surf.at[gz]
    strip[HALF : HALF + cols, :] = residual_ref[...] * whitening_ref[...]

    small[2].wait()
    small[3].wait()
    cell = (
        (gx * cols + lax.broadcasted_iota(jnp.int32, (cols, rows), 0)) * rows
        + lax.broadcasted_iota(jnp.int32, (cols, rows), 1)
    )

    def drill(i, top):
        return jnp.where(cell == wells_ref[i], FAR, top)

    top = lax.fori_loop(
        0, wells_ref.shape[0], drill, top_ref[...].astype(jnp.float32), unroll=16
    )
    x_id = lax.broadcasted_iota(jnp.int32, (cols, rows), 0)
    y_id = lax.broadcasted_iota(jnp.int32, (cols, rows), 1)
    tops[0] = top
    top_out[...] = top
    tops[1] = jnp.where(x_id == cols - 1, FAR, jnp.maximum(top, pltpu.roll(top, cols - 1, 0)))
    tops[2] = jnp.where(y_id == rows - 1, FAR, jnp.maximum(top, pltpu.roll(top, rows - 1, 1)))
    send_top[0] = jnp.broadcast_to(top[0:1, :], (8, rows))
    send_top[1] = jnp.broadcast_to(top[cols - 1 : cols, :], (8, rows))

    small[4].wait()
    kpad[...] = jnp.zeros(kpad.shape, jnp.float32)
    kpad[:, 0 : SIDE * SIDE] = kernel_ref[...]
    for x in range(8):
        put(toep, pl.ds(x, depth, stride=8), pltpu.roll(kpad[...], SIDE * x, 1))
    tail = shifted.shape[1] - (cols + 2 * HALF) * SIDE
    put(shifted, pl.ds((cols + 2 * HALF) * SIDE, tail), jnp.zeros((tail, rows), jnp.float32))

    def halve(i):
        tile = pl.ds(pl.multiple_of(i * 64, 64), 64)
        piece = get(toep, tile)
        hi = piece.astype(jnp.bfloat16)
        toep_hi[tile, :] = hi
        toep_lo[tile, :] = (piece - hi.astype(jnp.float32)).astype(jnp.bfloat16)

    every(0, depth * 8 // 64, 4, halve)

    tile = rows // 2
    k_id = lax.broadcasted_iota(jnp.int32, (rows, tile), 0)
    n_id = lax.broadcasted_iota(jnp.int32, (rows, tile), 1)
    same, nearby = k_id == n_id, k_id == n_id + 1
    pair_sum[...] = jnp.where(same, 1.0, jnp.where(nearby, 1.0, 0.0)).astype(jnp.bfloat16)
    same, nearby = k_id == n_id + tile, k_id + 1 == n_id + tile
    pair_step[...] = jnp.where(same, 1.0, jnp.where(nearby, -1.0, 0.0)).astype(jnp.bfloat16)

    block = 16 * cols

    def product_of(lhs, rhs):
        return jnp.dot(lhs, rhs, preferred_element_type=jnp.float32)

    def mobilities(i):
        at = pl.ds(pl.multiple_of(i * block, block), block)
        m = (0.5 * STEP_SIZE) * jnp.exp(get(logk, at))
        put(mob, at, m)
        m = m.astype(jnp.bfloat16)
        face_y[at, :tile] = product_of(m, pair_sum[...])
        face_y[at, tile:] = product_of(m[:, tile:], pair_sum[:tile, :])

    def flux_steps(i):
        at = pl.ds(pl.multiple_of(i * block, block), block)
        f = fy_narrow[at, :]
        flux_y[at, :tile] = product_of(f[:, :tile], pair_step[tile:, :])
        flux_y[at, tile:] = product_of(f, pair_step[...])

    for c in reversed(range(CHUNKS)):
        for copy in chunk_loads[c][: 2 * bands]:
            copy.wait()
        every(c * span // block, (c + 1) * span // block, 4, mobilities)

    strips_beside = jnp.where(has[0], 1, 0) + jnp.where(has[1], 1, 0)
    pl.semaphore_wait(barrier, n_gz - 1 + strips_beside)

    def surf_copy(j):
        mine = surf.at[gz, pl.ds(HALF, cols), :]
        return pltpu.make_async_remote_copy(
            src_ref=mine,
            dst_ref=mine,
            send_sem=surf_send.at[j - 1],
            recv_sem=surf_recv.at[j - 1],
            device_id=(gx, lax.rem(gz + j, n_gz)),
            device_id_type=MESH,
        )

    def surf_arrival(j):
        theirs = surf.at[lax.rem(gz + n_gz - j, n_gz), pl.ds(HALF, cols), :]
        return pltpu.make_async_remote_copy(
            src_ref=theirs,
            dst_ref=theirs,
            send_sem=surf_send.at[j - 1],
            recv_sem=surf_recv.at[j - 1],
            device_id=(gx, lax.rem(gz + j, n_gz)),
            device_id_type=MESH,
        )

    for j in range(1, n_gz):
        surf_copy(j).start()

    def pack(i):
        z0 = pl.multiple_of(i * 16, 16)
        r0 = pl.multiple_of(i * 16 * cols, 16 * cols)
        for s in range(2):
            line = pl.ds(r0 + s * (cols - 1), 16, stride=cols)
            fields = (get(adj, line), get(mob, line))
            near_adj[0, s, pl.ds(z0, 16), :] = fields[0]
            near_mob[s, pl.ds(z0, 16), :] = fields[1]
            for k, field in enumerate(fields):
                send_halo[s, pl.ds(k * depth + z0, 16), :] = field.astype(jnp.bfloat16)

    every(0, depth // 16, 2, pack)

    def swap(sent, arrived, send_sem, recv_sem):
        def leave(s):
            return pltpu.make_async_remote_copy(
                src_ref=sent.at[s],
                dst_ref=arrived.at[1 - s],
                send_sem=send_sem.at[s],
                recv_sem=recv_sem.at[1 - s],
                device_id=(beside[s], gz),
                device_id_type=MESH,
            )

        def come(s):
            return pltpu.make_async_remote_copy(
                src_ref=sent.at[1 - s],
                dst_ref=arrived.at[s],
                send_sem=send_sem.at[1 - s],
                recv_sem=recv_sem.at[s],
                device_id=(beside[s], gz),
                device_id_type=MESH,
            )

        return leave, come

    top_leave, top_come = swap(send_top, recv_top, top_send, top_recv)
    halo_leave, halo_come = swap(send_halo, recv_halo, halo_send, halo_recv)
    prs_leave, prs_come = swap(send_prs, recv_prs, prs_send, prs_recv)
    mid_leave, mid_come = swap(send_mid, recv_mid, mid_send, mid_recv)

    for s in range(2):

        @pl.when(has[s])
        def _():
            top_leave(s).start()
            halo_leave(s).start()

    z_base = gz * depth

    def next_x(ref, at):
        return get(ref, pl.ds(at + 1, cols))

    def next_y(value):
        return pltpu.roll(value, rows - 1, 1)

    def lower(at):
        return pl.ds(pl.multiple_of(at + 8, 8), cols)

    def lateral(level, a, a_next, at, open_x, open_y):
        here = pl.ds(at, cols)
        put(fx, lower(at), open_x * (a_next - a))
        dy = next_y(a) - a
        steps_y[level, here, :] = dy
        fy_narrow[here, :] = (open_y * dy).astype(jnp.bfloat16)

    def level_first(i, decay):
        z = depth - 1 - i
        at = pl.multiple_of(z * cols, cols)
        here = pl.ds(at, cols)
        zf = (z_base + z).astype(jnp.float32)
        open_x = jnp.where(tops[1] <= zf, get(mob, here) + next_x(mob, at), 0.0)
        open_y = jnp.where(tops[2] <= zf, face_y[here, :], 0.0)
        tx[here, :] = open_x
        ty[here, :] = open_y
        lateral(0, get(adj, here), next_x(adj, at), at, open_x, open_y)
        r = jnp.where(tops[0] <= zf, 1.0 / (1.0 + ver[here, :].astype(jnp.float32)), 0.0)
        rec[here, :] = r
        decay = decay - r * decay
        put(dec, here, decay)
        return decay

    decay = jnp.ones((cols, rows), jnp.float32)
    for c in range(CHUNKS):
        chunk_loads[c][2 * bands].wait()
    decay = lax.fori_loop(0, SPLIT, level_first, decay, unroll=UNROLL)

    def edge_copy(s):
        first = HALF + s * (cols - HALF)
        return pltpu.make_async_remote_copy(
            src_ref=surf.at[:, pl.ds(first, HALF), :],
            dst_ref=surf.at[:, pl.ds((1 - s) * (HALF + cols), HALF), :],
            send_sem=edge_send.at[s],
            recv_sem=edge_recv.at[1 - s],
            device_id=(beside[s], gz),
            device_id_type=MESH,
        )

    def edge_arrival(s):
        first = HALF + (1 - s) * (cols - HALF)
        return pltpu.make_async_remote_copy(
            src_ref=surf.at[:, pl.ds(first, HALF), :],
            dst_ref=surf.at[:, pl.ds(s * (HALF + cols), HALF), :],
            send_sem=edge_send.at[1 - s],
            recv_sem=edge_recv.at[s],
            device_id=(beside[s], gz),
            device_id_type=MESH,
        )

    for j in range(1, n_gz):
        surf_arrival(j).wait_recv()
    for s in range(2):

        @pl.when(has[s])
        def _():
            edge_copy(s).start()

    lax.fori_loop(SPLIT, depth, level_first, decay, unroll=UNROLL)
    every(0, cells // block, 4, flux_steps)

    def side_steps(level, s, i):
        z0 = pl.multiple_of(i * 16, 16)
        part = pl.ds(z0, 16)
        x = s * (cols - 1)
        zf = (z_base + z0 + lax.broadcasted_iota(jnp.int32, (16, rows), 0)).astype(jnp.float32)
        far = (recv_halo if level == 0 else recv_mid)[s, part, :].astype(jnp.float32)
        face = jnp.maximum(tops[0, x : x + 1, :], recv_top[s, 0:1, :])
        return part, jnp.where(face <= zf, far - near_adj[level, s, part, :], 0.0)

    def edges(level):
        def step(i):
            for s in range(2):
                part, d = side_steps(level, s, i)
                far_m = recv_halo[s, pl.ds(pl.multiple_of(depth + i * 16, 16), 16), :]
                put(edge_flux.at[s], part, (near_mob[s, part, :] + far_m.astype(jnp.float32)) * d)

        every(0, depth // 16, 4, step)

    def edge_terms():
        def step(i):
            for s in range(2):
                total = None
                for level in range(2):
                    part, d = side_steps(level, s, i)
                    p_part = pl.ds(pl.multiple_of(level * depth + i * 16, 16), 16)
                    far_p = recv_prs[s, p_part, :].astype(jnp.float32)
                    term = d * (far_p - send_prs[s, p_part, :].astype(jnp.float32))
                    total = term if total is None else total + term
                put(edge_term.at[s], part, total)

        every(0, depth // 16, 4, step)

    def pressure_steps(level, z, at):
        zf = (z_base + z).astype(jnp.float32)
        p = prs[pl.ds(pl.multiple_of(level * cells + at, cols), cols), :].astype(jnp.float32)
        across = jnp.where(tops[1] <= zf, pltpu.roll(p, cols - 1, 0) - p, 0.0)
        return across, jnp.where(tops[2] <= zf, next_y(p) - p, 0.0)

    def prepare_terms(z):
        at = pl.multiple_of(z * cols, cols)
        across, along = pressure_steps(1, z, at)
        step_x[pl.ds(at, cols), :] = across
        step_y[pl.ds(at, cols), :] = along

    def face_terms(level, add, ready):
        state = (adj, mid)[level]

        def step(z):
            at = pl.multiple_of(z * cols, cols)
            here = pl.ds(at, cols)
            if ready:
                across, along = step_x[here, :], step_y[here, :]
            else:
                across, along = pressure_steps(level, z, at)
            term_x = (next_x(state, at) - get(state, here)) * across
            term_y = steps_y[level, here, :] * along
            if add:
                term_x = term_x + get(gx_part, lower(at))
                term_y = term_y + gy_part[here, :]
                gy_sum[here, :] = term_y + pltpu.roll(term_y, 1, 1)
            else:
                gy_part[here, :] = term_y
            put(gx_sum if add else gx_part, lower(at), term_x)

        every(0, depth, UNROLL, step)

    def pack_pressures():
        z_of = lax.broadcasted_iota(jnp.int32, (32, 256), 0)
        k_of = lax.broadcasted_iota(jnp.int32, (32, 256), 1)
        pick = (k_of == jnp.where(z_of < 16, z_of * cols, z_of * cols - 15 * cols - 1)).astype(
            jnp.bfloat16
        )

        def step(i):
            block = prs[pl.ds(pl.multiple_of(i * 256, 256), 256), :]
            lines = jnp.dot(pick, block, preferred_element_type=jnp.float32).astype(jnp.bfloat16)
            part = pl.ds(pl.multiple_of(i * 16, 16), 16)
            send_prs[0, part, :] = lines[:16, :]
            send_prs[1, part, :] = lines[16:, :]

        every(0, 2 * depth // 16, 4, step)
    load_prs.wait()
    pack_pressures()

    def shift_rows(first, count):
        part = jnp.concatenate([surf[g, first : first + count, :] for g in range(n_gz)], axis=1)
        wide_y = lax.broadcasted_iota(jnp.int32, part.shape, 1)
        for b in range(SIDE):
            off = b - HALF
            turned = part if off == 0 else pltpu.roll(part, (-off) % rows, 1)
            if off > 0:
                turned = jnp.where(wide_y < rows - off, turned, 0.0)
            if off < 0:
                turned = jnp.where(wide_y >= -off, turned, 0.0)
            put(shifted, pl.ds(first * SIDE + b, count, stride=SIDE), turned)

    shift_rows(HALF, cols)
    for s in range(2):

        @pl.when(has[s])
        def _():
            edge_arrival(s).wait_recv()
            prs_leave(s).start()

    for s in range(2):
        shift_rows(s * (HALF + cols), HALF)
    for h in range(2):
        for q in range(4):
            piece = get(shifted, pl.ds(h * 8 * SIDE + q * 128, 128))
            hi = piece.astype(jnp.bfloat16)
            rhs_hi[h, pl.ds(q * 128, 128), :] = hi
            rhs_lo[h, pl.ds(q * 128, 128), :] = (piece - hi.astype(jnp.float32)).astype(
                jnp.bfloat16
            )

    def product(i):
        tile = pl.ds(pl.multiple_of(i * 256, 256), 256)
        for h in range(2):
            src[h, tile, :] = (
                jnp.dot(toep_hi[tile, :], rhs_hi[h], preferred_element_type=jnp.float32)
                + jnp.dot(toep_hi[tile, :], rhs_lo[h], preferred_element_type=jnp.float32)
                + jnp.dot(toep_lo[tile, :], rhs_hi[h], preferred_element_type=jnp.float32)
            )

    every(0, depth * 8 // 256, 2, product)

    def chain(state, i, below):
        z = depth - 1 - i
        eight = pl.ds(pl.multiple_of(z * 8, 8), 8)
        solved = []
        for h in range(2):
            at = pl.multiple_of(z * cols + 8 * h, 8)
            part = pl.ds(at, 8)
            across = get(fx, pl.ds(pl.multiple_of(at + 8, 8), 8)) - get(fx, pl.ds(at + 7, 8))
            e = (get(state, part) + flux_y[part, :]) + (across + src[h, eight, :])
            e = e + edge_rows(edge_flux, z, h, rows)
            v = below[h] + rec[part, :] * (e - below[h])
            put(low, part, v)
            solved.append(v)
        return tuple(solved)

    for s in range(2):

        @pl.when(has[s])
        def _():
            top_come(s).wait_recv()
            halo_come(s).wait_recv()

    edges(0)
    nothing = (jnp.zeros((8, rows), jnp.float32),) * 2
    lax.fori_loop(0, depth, functools.partial(chain, adj), nothing, unroll=4)

    def inc_copy(level, to):
        return pltpu.make_async_remote_copy(
            src_ref=send_inc.at[level],
            dst_ref=recv_inc.at[level],
            send_sem=inc_send.at[level],
            recv_sem=inc_recv.at[level],
            device_id=(gx, to),
            device_id_type=MESH,
        )

    def relay(level):
        @pl.when(gz < n_gz - 1)
        def _():
            inc_copy(level, gz + 1).wait_recv()

        @pl.when(gz > 0)
        def _():
            first = pl.ds(0, cols)
            send_inc[level] = get(low, first) + get(dec, first) * recv_inc[level]
            inc_copy(level, gz - 1).start()

    early = gz < n_gz // 2

    @pl.when(early)
    def _():
        face_terms(0, False, False)
        every(0, depth, UNROLL, prepare_terms)

    relay(0)

    def pack_mid(i):
        z0 = pl.multiple_of(i * 16, 16)
        r0 = pl.multiple_of(i * 16 * cols, 16 * cols)
        for s in range(2):
            x = s * (cols - 1)
            line = pl.ds(r0 + x, 16, stride=cols)
            value = get(low, line) + get(dec, line) * recv_inc[0, x : x + 1, :]
            near_adj[1, s, pl.ds(z0, 16), :] = value
            send_mid[s, pl.ds(z0, 16), :] = value.astype(jnp.bfloat16)

    every(0, depth // 16, 4, pack_mid)

    for s in range(2):

        @pl.when(has[s])
        def _():
            mid_leave(s).start()

    below_next = pltpu.roll(recv_inc[0], cols - 1, 0)

    def level_second(z):
        at = pl.multiple_of(z * cols, cols)
        here = pl.ds(at, cols)
        a = get(low, here) + get(dec, here) * recv_inc[0]
        a_next = next_x(low, at) + next_x(dec, at) * below_next
        put(mid, here, a)
        lateral(1, a, a_next, at, tx[here, :], ty[here, :])

    every(0, depth, UNROLL, level_second)
    every(0, cells // block, 4, flux_steps)

    @pl.when(early)
    def _():
        face_terms(1, True, True)

    @pl.when(jnp.logical_not(early))
    def _():
        face_terms(1, False, False)

    for s in range(2):

        @pl.when(has[s])
        def _():
            mid_come(s).wait_recv()

    edges(1)
    lax.fori_loop(0, depth, functools.partial(chain, mid), nothing, unroll=4)
    relay(1)

    @pl.when(jnp.logical_not(early))
    def _():
        face_terms(0, True, False)

    for s in range(2):

        @pl.when(has[s])
        def _():
            prs_come(s).wait_recv()

    edge_terms()

    inc_ref[...] = recv_inc[1]

    for j in range(1, n_gz):
        surf_copy(j).wait_send()
    for s in range(2):

        @pl.when(has[s])
        def _():
            top_leave(s).wait_send()
            halo_leave(s).wait_send()
            prs_leave(s).wait_send()
            edge_copy(s).wait_send()
            mid_leave(s).wait_send()

    @pl.when(gz > 0)
    def _():
        inc_copy(0, gz - 1).wait_send()
        inc_copy(1, gz - 1).wait_send()


def on_device(
    n_gx,
    n_gz,
    residual,
    whitening,
    kernel,
    adjoint_end,
    pressure,
    log_permeability,
    vertical,
    top_layer,
    well_columns,
):
    depth, cols, rows = adjoint_end.shape
    cells = depth * cols
    f32, b16 = jnp.float32, jnp.bfloat16
    lanes = rows // LANES
    vmem = pltpu.VMEM
    field = vmem((cells, rows), f32)
    banded = vmem((lanes, cells + 8, LANES), f32)
    dma = pltpu.SemaphoreType.DMA
    wide = cols + 2 * HALF
    hbm = pl.BlockSpec(memory_space=pl.ANY)
    in_vmem = pl.BlockSpec(memory_space=vmem)
    kept = (
        banded,
        banded,
        vmem((cols, rows), f32),
        banded,
        field,
        banded,
        vmem((2, lanes, depth, LANES), f32),
        vmem((cols, rows), f32),
    )
    state = pl.pallas_call(
        functools.partial(window_kernel, n_gx, n_gz, depth, cols, rows),
        out_shape=kept,
        in_specs=[hbm] * 9,
        out_specs=(in_vmem,) * len(kept),
        scratch_shapes=[
            vmem(residual.shape, f32),
            vmem(whitening.shape, f32),
            vmem(kernel.shape, f32),
            vmem(top_layer.shape, jnp.int32),
            pltpu.SMEM(well_columns.shape, jnp.int32),
            banded,
            vmem((2 * cells, rows), b16),
            banded,
            vmem((cells, rows), b16),
            field,
            field,
            field,
            banded,
            vmem((cells, rows), b16),
            field,
            vmem((2, cells, rows), f32),
            banded,
            field,
            field,
            field,
            field,
            banded,
            vmem((2, depth * 8, rows), f32),
            vmem((n_gz, wide, rows // n_gz), f32),
            vmem((lanes, 8 * SIDE + 512, LANES), f32),
            vmem((2, 512, rows), b16),
            vmem((2, 512, rows), b16),
            vmem((depth, 512), f32),
            vmem((4, depth * 8, LANES), f32),
            vmem((depth * 8, 512), b16),
            vmem((depth * 8, 512), b16),
            vmem((3, cols, rows), f32),
            vmem((2, 2, depth, rows), f32),
            vmem((2, depth, rows), f32),
            vmem((2, lanes, depth, LANES), f32),
            vmem((rows, rows // 2), b16),
            vmem((rows, rows // 2), b16),
            vmem((2, 2 * depth, rows), b16),
            vmem((2, 2 * depth, rows), b16),
            vmem((2, 2 * depth, rows), b16),
            vmem((2, 2 * depth, rows), b16),
            vmem((2, 8, rows), f32),
            vmem((2, 8, rows), f32),
            vmem((2, depth, rows), b16),
            vmem((2, depth, rows), b16),
            vmem((2, cols, rows), f32),
            vmem((2, cols, rows), f32),
            dma((6,)),
            dma((CHUNKS, 1 + 2 * lanes)),
            dma((n_gz - 1,)),
            dma((n_gz - 1,)),
        ]
        + [dma((2,))] * 12,
        compiler_params=pltpu.CompilerParams(
            collective_id=0, has_side_effects=True, vmem_limit_bytes=50 * 1024 * 1024
        ),
    )(
        residual,
        whitening,
        kernel,
        top_layer,
        well_columns,
        adjoint_end.reshape(cells, rows),
        pressure.reshape(2 * cells, rows),
        log_permeability.reshape(cells, rows),
        vertical.reshape(cells, rows),
    )
    adjoint_start, gradient = pl.pallas_call(
        functools.partial(finish_kernel, n_gx, depth, cols, rows),
        out_shape=(jax.ShapeDtypeStruct((cells, rows), f32),) * 2,
        in_specs=[in_vmem] * len(kept),
        out_specs=(hbm, hbm),
        scratch_shapes=[field, field, dma((STORES, 2))],
        compiler_params=pltpu.CompilerParams(vmem_limit_bytes=8 * 1024 * 1024),
    )(*state)
    shape = (depth, cols, rows)
    return adjoint_start.reshape(shape), gradient.reshape(shape)


def solution(mesh):
    in_specs = (
        P("gx", "gz"),
        P("gx", "gz"),
        P("gz", None),
        P("gz", "gx", None),
        P(None, "gz", "gx", None),
        P("gz", "gx", None),
        P("gz", "gx", None),
        P("gx", None),
        P(),
    )
    out_specs = (P("gz", "gx", None), P("gz", "gx", None))
    return jax.shard_map(
        functools.partial(on_device, mesh.shape["gx"], mesh.shape["gz"]),
        mesh=mesh,
        in_specs=in_specs,
        out_specs=out_specs,
        check_vma=False,
    )
```
